32 devices in a mesh: ctx: 8 (over z, x), tp: 4 (over y, core).
Axes of the slice: x: 2, y: 2, z: 4, core: 2. Of those that a mesh axis runs over, the one named last changes fastest.
Arguments:
- layer_input: bfloat16 [4096, 1536], P('ctx'), may hold values from -6 to 6
- segment_ids: int32 [4096], P('ctx'), may hold values from 0 to 3, as said below
- positions: int32 [4096], P('ctx'), may hold values from 0 to 4095, as said below
- attn_gain: bfloat16 [1536], replicated, may hold values from 0.5 to 1.5
- q_weight: bfloat16 [1536, 1536], P(None, 'tp'), may hold values from -0.15625 to 0.15625
- q_bias: bfloat16 [12, 128], P('tp'), may hold values from -3 to 3
- kv_weight: bfloat16 [1536, 512], replicated, may hold values from -0.15625 to 0.15625
- kv_bias: bfloat16 [512], replicated, may hold values from -0.59765625 to 0.59765625
- o_weight: bfloat16 [1536, 1536], P('tp'), may hold values from -1 to 1
- mlp_gain: bfloat16 [1536], replicated, may hold values from 0.5 to 1.5
- gate_weight: bfloat16 [1536, 8960], P(None, 'tp'), may hold values from -0.15625 to 0.15625
- up_weight: bfloat16 [1536, 8960], P(None, 'tp'), may hold values from -0.15625 to 0.15625
- down_weight: bfloat16 [8960, 1536], P('tp'), may hold values from -0.0625 to 0.0625
- cotangent: bfloat16 [4096, 1536], P('ctx'), may hold values from -6 to 6
Outputs:
- layer_output: bfloat16 [4096, 1536], P('ctx')
- dx: float32 [4096, 1536], P('ctx')
- g_attn_gain: float32 [1536], P('ctx')
- g_q_weight: float32 [1536, 1536], P('ctx', 'tp')
- g_q_bias: float32 [12, 128], P('tp', 'ctx')
- g_kv_weight: float32 [1536, 512], P(('ctx', 'tp'))
- g_kv_bias: float32 [512], P(('ctx', 'tp'))
- g_o_weight: float32 [1536, 1536], P('tp', 'ctx')
- g_mlp_gain: float32 [1536], P('ctx')
- g_gate_weight: float32 [1536, 8960], P('ctx', 'tp')
- g_up_weight: float32 [1536, 8960], P('ctx', 'tp')
- g_down_weight: float32 [8960, 1536], P('tp', 'ctx')
The draws below stay inside these ranges and needn't reach their ends.
Inputs may be any that keep to these rules, and one draw needn't show every extreme that they name: `segment_ids`: segment ids never fall along the row and number four documents: document 0 and documents 2 and 3 hold 1 to 128 tokens each, document 1 holds all the others. Within a document the positions rise by one from token to token; document 0 starts at 0, documents 2 and 3 at an offset below 1024, and the positions of document 1 end at 4095.
All inputs are finite; a program needn't handle non-finite values.
Results may differ from the reference program's by a relative error of at most 0.02.
Values may be sent and summed in bfloat16 or wider, within the bound.
No kernel may reach another device: no remote copies, remote signals or barrier semaphores. Data moves between devices by JAX's collectives and lax.ppermute only.
A program may use at most 192 MiB of HBM per device.

```python
import jax
import jax.numpy as jnp
from jax import lax

D = 1536
H = 12
KVH = 2
HD = 128
FF = 8960
TOK_DEV = 512
TOKENS = 4096
N_TP = 4


def row_layout(key):
    base = jax.random.fold_in(key, 11)
    parts = jax.random.split(base, 4)
    quarter = TOK_DEV // 4
    first_len = jax.random.randint(parts[0], (), 1, quarter + 1, dtype=jnp.int32)
    third_len = jax.random.randint(parts[1], (), 1, quarter + 1, dtype=jnp.int32)
    fourth_len = jax.random.randint(parts[2], (), 1, quarter + 1, dtype=jnp.int32)
    short_top = min(1024, TOKENS - quarter)
    short_offsets = jax.random.randint(parts[3], (2,), 0, short_top, dtype=jnp.int32)
    long_offset = (first_len + third_len + fourth_len).astype(jnp.int32)
    offsets = jnp.concatenate([jnp.zeros((1,), jnp.int32), long_offset[None], short_offsets])
    token_index = jnp.arange(TOKENS, dtype=jnp.int32)
    starts = jnp.stack([jnp.zeros((), jnp.int32), first_len, TOKENS - third_len - fourth_len, TOKENS - fourth_len]).astype(jnp.int32)
    segment = jnp.sum((token_index[:, None] >= starts[None, 1:]).astype(jnp.int32), axis=-1)
    member = (segment[:, None] == jnp.arange(4, dtype=jnp.int32)[None, :]).astype(jnp.int32)
    own_start = jnp.sum(member * starts[None, :], axis=-1)
    own_offset = jnp.sum(member * offsets[None, :], axis=-1)
    return (segment, token_index - own_start + own_offset)


def draw_segment_ids(key, part):
    return row_layout(key)[0]


def draw_positions(key, part):
    return row_layout(key)[1]


def level_of(key, dims, cuts, low, high):
    def one(dim, blocks):
        heights = jax.random.uniform(jax.random.fold_in(jax.random.fold_in(key, 6), dim), (blocks,), jnp.float32, low / len(cuts), high / len(cuts))
        return jnp.repeat(jnp.exp(heights), dims[dim] // blocks).reshape((-1,) + (1,) * (len(dims) - dim - 1))

    factor_of = one(*cuts[0])
    for cut in cuts[1:]:
        factor_of = factor_of * one(*cut)
    return factor_of


def noise(rng, dims, deviation, bound, pieces=(), kind=jnp.bfloat16):
    values = jax.random.normal(rng, dims, jnp.float32) * deviation
    if len(pieces) > 0:
        values = level_of(rng, dims, pieces, -0.22, 0.18) * values
    return jnp.clip(values, min=-bound, max=bound).astype(kind)


def setup_inputs(seed: int = 0) -> dict:
    streams_of = jax.random.split(jax.random.key(seed), 15)
    return {
        "layer_input": noise(streams_of[0], (TOKENS, D), 1.0, 6.0, ((0, 8),)),
        "segment_ids": draw_segment_ids(jax.random.fold_in(streams_of[14], 71), 0),
        "positions": draw_positions(jax.random.fold_in(streams_of[14], 71), 0),
        "attn_gain": jnp.clip(1.0 + 0.1 * jax.random.normal(streams_of[3], (D,), jnp.float32), 0.5, 1.5).astype(jnp.bfloat16),
        "q_weight": noise(streams_of[4], (D, H * HD), D ** -0.5, 0.15625, ((1, 4),)),
        "q_bias": noise(streams_of[5], (H, HD), 0.5, 3.0, ((0, 4),)),
        "kv_weight": noise(streams_of[6], (D, 2 * KVH * HD), D ** -0.5, 0.15625),
        "kv_bias": noise(streams_of[7], (2 * KVH * HD,), 0.1, 0.59765625),
        "o_weight": noise(streams_of[8], (H * HD, D), 32 ** -0.5, 1.0, ((0, 4),)),
        "mlp_gain": jnp.clip(1.0 + 0.1 * jax.random.normal(streams_of[9], (D,), jnp.float32), 0.5, 1.5).astype(jnp.bfloat16),
        "gate_weight": noise(streams_of[10], (D, FF), D ** -0.5, 0.15625, ((1, 4),)),
        "up_weight": noise(streams_of[11], (D, FF), D ** -0.5, 0.15625, ((1, 4),)),
        "down_weight": noise(streams_of[12], (FF, D), FF ** -0.5, 0.0625, ((0, 4),)),
        "cotangent": noise(streams_of[13], (TOKENS, D), 1.0, 6.0, ((0, 8),)),
    }


rms_eps = 1e-06
rope_base = 1000000.0
masked_score = -1000000000.0

@jax.custom_vjp
def low(v):
    return lax.optimization_barrier(v.astype(jnp.bfloat16)).astype(jnp.float32)

@jax.custom_vjp
def low_back(v):
    return v

def low_keep(v):
    return (low(v), None)

def low_pass(kept, grad):
    return (grad,)

def back_keep(v):
    return (v, None)

def back_low(kept, grad):
    return (low(grad),)
low.defvjp(low_keep, low_pass)
low_back.defvjp(back_keep, back_low)

def rms_norm(values, gain):
    factor = lax.rsqrt(lax.optimization_barrier(jnp.mean(values * values, axis=-1, keepdims=True)) + rms_eps)
    return values * factor * gain

def rotate(values, positions):
    half_width = values.shape[-1] // 2
    steps_up = jnp.arange(half_width, dtype=jnp.float32)
    freqs = rope_base ** (-2.0 * steps_up / values.shape[-1])
    angles = positions.astype(jnp.float32)[:, None] * freqs[None, :]
    cosine = jnp.cos(angles)[:, None, :]
    sine = jnp.sin(angles)[:, None, :]
    first_half = values[..., :half_width]
    second_half = values[..., half_width:]
    return jnp.concatenate([first_half * cosine - second_half * sine, second_half * cosine + first_half * sine], axis=-1)

def attention(query_rot, key_groups, value_groups, segment_ids):
    tokens, heads, head_dim = query_rot.shape
    groups = key_groups.shape[0]
    per_group = heads // groups
    block = min(128, TOK_DEV)
    count = tokens // block
    token_index = jnp.arange(tokens, dtype=jnp.int32)
    queries = query_rot.reshape(count, block, groups, per_group, head_dim)
    query_index = token_index.reshape(count, block)
    query_seg = segment_ids.reshape(count, block)

    def one_block(block_item):
        query_block, block_index, block_seg = block_item
        scores = jnp.einsum('bgld,gkd->bglk', query_block, key_groups, precision=lax.Precision.HIGHEST) * head_dim ** (-0.5)
        scores = low_back(scores)
        allowed = (token_index[None, :] <= block_index[:, None]) & (segment_ids[None, :] == block_seg[:, None])
        weights = jnp.exp(jnp.where(allowed[:, None, None, :], scores, masked_score))
        totals = lax.optimization_barrier(jnp.sum(weights, axis=-1))
        weighted = low_back(jnp.einsum('bglk,gkd->bgld', low(weights), value_groups, precision=lax.Precision.HIGHEST))
        return low(weighted / totals[..., None]).reshape(block, heads * head_dim)
    attended = lax.map(jax.checkpoint(one_block), (queries, query_index, query_seg))
    return attended.reshape(tokens, heads * head_dim)

def layer(layer_input, attn_gain, q_weight, q_bias, kv_weight, kv_bias, o_weight, mlp_gain, gate_weight, up_weight, down_weight, segment_ids, positions):
    tokens = layer_input.shape[0]
    heads, head_dim = q_bias.shape
    kv_heads = kv_bias.shape[0] // (2 * head_dim)
    per_group = heads // N_TP
    sharing = heads // kv_heads
    normed = low(rms_norm(layer_input, attn_gain))
    query = low_back(jnp.dot(normed, q_weight, precision=lax.Precision.HIGHEST) + q_bias.reshape(-1))
    query_rot = low(rotate(query.reshape(tokens, heads, head_dim), positions))
    key_value = jnp.dot(normed, kv_weight, precision=lax.Precision.HIGHEST) + kv_bias
    key_list = []
    value_list = []
    for member in range(N_TP):
        head_number = member * per_group // sharing
        key_part = low_back(key_value[:, head_number * head_dim:(head_number + 1) * head_dim])
        key_list.append(low(rotate(key_part[:, None, :], positions)[:, 0, :]))
        value_first = (kv_heads + head_number) * head_dim
        value_list.append(low(low_back(key_value[:, value_first:value_first + head_dim])))
    attended = attention(query_rot, jnp.stack(key_list), jnp.stack(value_list), segment_ids)
    hidden_in = layer_input + low_back(jnp.dot(attended, o_weight, precision=lax.Precision.HIGHEST))
    normed_two = low(rms_norm(hidden_in, mlp_gain))
    gate = low_back(jnp.dot(normed_two, gate_weight, precision=lax.Precision.HIGHEST))
    up_proj = low_back(jnp.dot(normed_two, up_weight, precision=lax.Precision.HIGHEST))
    hidden = low(jax.nn.silu(gate) * up_proj)
    return hidden_in + jnp.dot(hidden, down_weight, precision=lax.Precision.HIGHEST)

def reference(layer_input, segment_ids, positions, attn_gain, q_weight, q_bias, kv_weight, kv_bias, o_weight, mlp_gain, gate_weight, up_weight, down_weight, cotangent):
    floats = tuple((item.astype(jnp.float32) for item in (layer_input, attn_gain, q_weight, q_bias, kv_weight, kv_bias, o_weight, mlp_gain, gate_weight, up_weight, down_weight)))

    def forward(*weights_in):
        return layer(*weights_in, segment_ids, positions)
    result, pull = jax.vjp(forward, *floats)
    grads = pull(cotangent.astype(jnp.float32))
    return (result.astype(jnp.bfloat16), grads[0], grads[1], grads[2], grads[3], grads[4], grads[5], grads[6], grads[7], grads[8], grads[9], grads[10])
```

```python
import functools

import jax
import jax.numpy as jnp
from jax import lax
from jax.experimental import pallas as pl
from jax.experimental.pallas import tpu as pltpu
from jax.sharding import PartitionSpec as P

RMS_EPS = 1e-06
ROPE_BASE = 1000000.0
LOG2E = 1.4426950408889634
BF16 = jnp.bfloat16
F32 = jnp.float32
EXTRA = 16


def mm(a, b, ca, cb):
    return lax.dot_general(a, b, (((ca,), (cb,)), ((), ())), preferred_element_type=F32)


def rope_tables(positions, head_dim):
    half = head_dim // 2
    freqs = ROPE_BASE ** (-2.0 * jnp.arange(half, dtype=F32) / head_dim)
    angles = positions.astype(F32)[:, None] * freqs[None, :]
    return jnp.cos(angles), jnp.sin(angles)


def rotate(values, cosine, sine):
    half = cosine.shape[-1]
    first, second = values[..., :half], values[..., half:]
    return jnp.concatenate([first * cosine - second * sine, second * cosine + first * sine], axis=-1)


def swap_core(x):
    return lax.ppermute(x, "tp", [(0, 1), (1, 0), (2, 3), (3, 2)])


def swap_y(x):
    return lax.ppermute(x, "tp", [(0, 2), (2, 0), (1, 3), (3, 1)])


def gather_tp(x, core, y):
    mate = swap_core(x)
    far = swap_y(x)
    far_mate = swap_core(far)
    a0, a1 = jnp.where(core == 0, x, mate), jnp.where(core == 0, mate, x)
    b0, b1 = jnp.where(core == 0, far, far_mate), jnp.where(core == 0, far_mate, far)
    return [
        jnp.where(y == 0, a0, b0),
        jnp.where(y == 0, a1, b1),
        jnp.where(y == 0, b0, a0),
        jnp.where(y == 0, b1, a1),
    ]


def sum_tp(part, core):
    rows = part.shape[0] // 2
    keep = lax.dynamic_slice_in_dim(part, core * rows, rows, 0)
    give = lax.dynamic_slice_in_dim(part, (1 - core) * rows, rows, 0).astype(BF16)
    half = (keep + swap_core(give).astype(F32)).astype(BF16)
    half = (half.astype(F32) + swap_y(half).astype(F32)).astype(BF16)
    mate = swap_core(half)
    return jnp.concatenate([jnp.where(core == 0, half, mate), jnp.where(core == 0, mate, half)], axis=0)


def sum_scatter(parts):
    got = lax.all_to_all(parts, "ctx", split_axis=0, concat_axis=0, tiled=True)
    return jnp.sum(got.astype(F32), axis=0)


def block_bounds(scal, rows):
    return lax.div(scal[1], rows), scal[0] + 1


def probs_t(scal, kb, qh, lo_row, b, rows, factor, shift, masked):
    s = mm(kb, qh, 1, 1) * factor
    if shift is not None:
        s = s - shift
    p = jnp.exp2(s)
    if masked:
        key = b * rows + lax.broadcasted_iota(jnp.int32, p.shape, 0)
        query = scal[0] * p.shape[1] + lax.broadcasted_iota(jnp.int32, p.shape, 1)
        p = jnp.where((key <= query) & (key >= lo_row), p, 0.0)
    return p


def for_blocks(scal, rows, run):
    start, stop = block_bounds(scal, rows)

    def body(b, carry):
        plain = (b < scal[0]) & (scal[2] <= b * rows)

        @pl.when(plain)
        def _():
            run(b, False)

        @pl.when(jnp.logical_not(plain))
        def _():
            run(b, True)

        return carry

    lax.fori_loop(start, stop, body, 0)


def attend_kernel(scal, q_ref, mine_ref, other_ref, lo_ref, att_ref, log_ref, acc, tot):
    rows, width = q_ref.shape
    hd = mine_ref.shape[2]
    heads = width // hd
    factor = LOG2E * hd**-0.5
    acc[...] = jnp.zeros_like(acc)
    tot[...] = jnp.zeros_like(tot)

    def run(b, masked):
        a = mine_ref[b, 0:rows, :]
        o = other_ref[b, 0:rows, :]
        kb = jnp.where(scal[3] == 0, a, o)
        vt = jnp.where(scal[3] == 0, o, a).astype(F32).T.astype(BF16)
        for h in range(heads):
            p = probs_t(
                scal, kb, q_ref[:, h * hd : (h + 1) * hd], lo_ref[...], b, rows, factor, None, masked
            )
            tot[h] += jnp.sum(p.reshape(rows // 8, 8, p.shape[1]), axis=0)
            acc[h] += mm(vt, p.astype(BF16), 1, 0)

    for_blocks(scal, rows, run)
    for h in range(heads):
        total = jnp.sum(tot[h], axis=0, keepdims=True)
        att_ref[:, h * hd : (h + 1) * hd] = (acc[h] / total).T.astype(BF16)
        log_ref[h] = jnp.broadcast_to(jnp.log2(total), log_ref.shape[1:])


def attend_back_kernel(
    scal, q_ref, mine_ref, other_ref, lo_ref, att_ref, log_ref, d_ref, dq_ref, dk_ref, dv_ref, acc, delta
):
    rows, width = q_ref.shape
    hd = mine_ref.shape[2]
    heads = width // hd
    scale = hd**-0.5
    factor = LOG2E * scale
    acc[...] = jnp.zeros_like(acc)
    for h in range(heads):
        cols = slice(h * hd, (h + 1) * hd)
        both = d_ref[:, cols].astype(F32) * att_ref[:, cols].astype(F32)
        delta[h] = jnp.broadcast_to(jnp.sum(both.T, axis=0, keepdims=True), delta.shape[1:])
    zero = jnp.zeros((rows, hd), BF16)

    def clear(b, carry):
        dk_ref[b] = zero
        dv_ref[b] = zero
        return carry

    start, stop = block_bounds(scal, rows)
    lax.fori_loop(0, start, clear, 0)
    lax.fori_loop(stop, dk_ref.shape[0], clear, 0)

    def run(b, masked):
        a = mine_ref[b, 0:rows, :]
        o = other_ref[b, 0:rows, :]
        kb = jnp.where(scal[3] == 0, a, o)
        vb = jnp.where(scal[3] == 0, o, a)
        kt = kb.astype(F32).T.astype(BF16)
        dk = jnp.zeros((rows, hd), F32)
        dv = jnp.zeros((rows, hd), F32)
        for h in range(heads):
            cols = slice(h * hd, (h + 1) * hd)
            qh = q_ref[:, cols]
            dh = d_ref[:, cols]
            p = probs_t(scal, kb, qh, lo_ref[...], b, rows, factor, log_ref[h, 0:1, :], masked)
            dp = mm(vb, dh, 1, 1)
            ds = (p * (dp - delta[h, 0:1, :])).astype(BF16)
            dv += mm(p.astype(BF16), dh, 1, 0)
            dk += mm(ds, qh, 1, 0)
            acc[h] += mm(kt, ds, 1, 0)
        dk_ref[b] = (dk * scale).astype(BF16)
        dv_ref[b] = dv.astype(BF16)

    for_blocks(scal, rows, run)
    for h in range(heads):
        dq_ref[:, h * hd : (h + 1) * hd] = (acc[h] * scale).T


VMEM = pl.BlockSpec(memory_space=pltpu.VMEM)
SMEM = pl.BlockSpec(memory_space=pltpu.SMEM)
LIMIT = 56 * 1024 * 1024


def attend(scal, q, mine, other, lo):
    rows, width = q.shape
    hd = mine.shape[2]
    heads = width // hd
    blocks = mine.shape[0]
    work = rows * width * rows * blocks
    return pl.pallas_call(
        attend_kernel,
        in_specs=[SMEM, VMEM, VMEM, VMEM, VMEM],
        out_specs=[VMEM, VMEM],
        out_shape=[
            jax.ShapeDtypeStruct((rows, width), BF16),
            jax.ShapeDtypeStruct((heads, 8, rows), F32),
        ],
        scratch_shapes=[pltpu.VMEM((heads, hd, rows), F32), pltpu.VMEM((heads, 8, rows), F32)],
        compiler_params=pltpu.CompilerParams(vmem_limit_bytes=LIMIT),
        cost_estimate=pl.CostEstimate(
            flops=4 * work, bytes_accessed=4 * mine.size, transcendentals=work // hd
        ),
        name="attend",
    )(scal, q, mine, other, lo)


def attend_back(scal, q, mine, other, lo, att, logs, d_att):
    rows, width = q.shape
    hd = mine.shape[2]
    heads = width // hd
    blocks = mine.shape[0]
    work = rows * width * rows * blocks
    grads = jax.ShapeDtypeStruct((blocks, rows, hd), BF16)
    return pl.pallas_call(
        attend_back_kernel,
        in_specs=[SMEM] + [VMEM] * 7,
        out_specs=[VMEM, VMEM, VMEM],
        out_shape=[jax.ShapeDtypeStruct((rows, width), F32), grads, grads],
        scratch_shapes=[pltpu.VMEM((heads, hd, rows), F32), pltpu.VMEM((heads, 8, rows), F32)],
        compiler_params=pltpu.CompilerParams(vmem_limit_bytes=LIMIT),
        cost_estimate=pl.CostEstimate(
            flops=10 * work, bytes_accessed=8 * mine.size, transcendentals=work // hd
        ),
        name="attend_back",
    )(scal, q, mine, other, lo, att, logs, d_att)


def per_device(
    layer_input,
    segment_ids,
    positions,
    attn_gain,
    q_weight,
    q_bias,
    kv_weight,
    kv_bias,
    o_weight,
    mlp_gain,
    gate_weight,
    up_weight,
    down_weight,
    cotangent,
):
    rows, width = layer_input.shape
    heads, hd = q_bias.shape
    ff = gate_weight.shape[1]
    n = lax.axis_size("ctx")
    ntp = lax.axis_size("tp")
    ctx = lax.axis_index("ctx")
    tp = lax.axis_index("tp")
    core = tp % 2
    y = tp // 2
    quarter = rows // ntp
    unit = ff // n

    o_full = lax.all_gather(o_weight, "tp", axis=0, tiled=True)
    q_full = lax.all_gather(q_weight.T, "tp", axis=0, tiled=True)
    cot_all = lax.all_gather(
        lax.dynamic_slice_in_dim(cotangent, tp * quarter, quarter, 0), ("ctx", "tp"), axis=0, tiled=True
    )
    gate_s = lax.dynamic_slice_in_dim(gate_weight, ctx * unit, unit, 1)
    up_s = lax.dynamic_slice_in_dim(up_weight, ctx * unit, unit, 1)
    down_s = lax.dynamic_slice_in_dim(down_weight, ctx * unit, unit, 0)

    inputs = layer_input.astype(F32)
    gain_one = attn_gain.astype(F32)
    factor_one = lax.rsqrt(jnp.mean(inputs * inputs, axis=-1, keepdims=True) + RMS_EPS)
    normed = (inputs * factor_one * gain_one).astype(BF16)
    cosine, sine = rope_tables(positions, hd)
    query = mm(normed, q_weight, 1, 0) + q_bias.astype(F32).reshape(-1)
    query_rot = rotate(query.reshape(rows, heads, hd), cosine[:, None], sine[:, None])
    query_rot = query_rot.astype(BF16).reshape(rows, heads * hd)
    column = (2 * core + y) * hd
    kv_cols = lax.dynamic_slice_in_dim(kv_weight, column, hd, 1)
    kv_own_bias = lax.dynamic_slice_in_dim(kv_bias, column, hd, 0).astype(F32)
    kv_own = mm(normed, kv_cols, 1, 0) + kv_own_bias
    kv_own = jnp.where(core == 0, rotate(kv_own, cosine, sine), kv_own).astype(BF16)

    ids = segment_ids.astype(BF16).reshape(rows // hd, hd)
    ids = jnp.pad(ids, ((0, EXTRA - rows // hd), (0, 0)))
    packed = jnp.concatenate([kv_own, ids], axis=0)
    mine = lax.all_to_all(
        jnp.broadcast_to(packed[None], (n,) + packed.shape), "ctx", split_axis=0, concat_axis=0, tiled=True
    )
    other = swap_core(mine)
    all_ids = mine[:, rows : rows + rows // hd, :].astype(F32)
    starts = [jnp.sum((all_ids < k).astype(F32)).astype(jnp.int32) for k in (1, 2, 3)]
    lo = jnp.where(
        segment_ids == 0,
        0,
        jnp.where(segment_ids == 1, starts[0], jnp.where(segment_ids == 2, starts[1], starts[2])),
    )
    scal = jnp.stack([ctx, lo[0], lo[-1], core]).astype(jnp.int32)
    lo = lo.reshape(1, rows)

    attended, logs = attend(scal, query_rot, mine, other, lo)
    attended_all = jnp.concatenate(gather_tp(attended, core, y), axis=1)
    hidden_in = inputs + mm(attended_all, o_full, 1, 0)

    gain_two = mlp_gain.astype(F32)
    factor_two = lax.rsqrt(jnp.mean(hidden_in * hidden_in, axis=-1, keepdims=True) + RMS_EPS)
    normed_two = (hidden_in * factor_two * gain_two).astype(BF16)
    normed_all = lax.all_gather(
        lax.dynamic_slice_in_dim(normed_two, tp * quarter, quarter, 0), ("ctx", "tp"), axis=0, tiled=True
    )

    gate = mm(normed_two, gate_weight, 1, 0)
    up = mm(normed_two, up_weight, 1, 0)
    d_hidden = mm(cotangent, down_weight, 1, 1)
    sig = jax.nn.sigmoid(gate)
    hidden = (gate * sig * up).astype(BF16)
    d_gate = (d_hidden * up * sig * (1.0 + gate * (1.0 - sig))).astype(BF16)
    d_up = (d_hidden * gate * sig).astype(BF16)
    d_normed_two = mm(d_gate, gate_weight, 1, 1) + mm(d_up, up_weight, 1, 1)
    d_normed_two = sum_tp(d_normed_two, core).astype(F32)
    mlp_part = mm(hidden, down_weight, 1, 0).astype(BF16)
    output = (hidden_in + lax.psum(mlp_part, "tp").astype(F32)).astype(BF16)

    w_two = hidden_in * factor_two
    part_mlp_gain = jnp.sum(d_normed_two * w_two, axis=0)
    dg_two = d_normed_two * gain_two
    d_hidden_in = cotangent.astype(F32) + factor_two * (
        dg_two - w_two * jnp.mean(dg_two * w_two, axis=-1, keepdims=True)
    )
    d_attn = d_hidden_in.astype(BF16)
    d_attended = mm(d_attn, o_weight, 1, 1).astype(BF16)

    d_query_rot, dk_all, dv_all = attend_back(scal, query_rot, mine, other, lo, attended, logs, d_attended)
    keep = jnp.where(core == 0, dk_all, dv_all)
    give = jnp.where(core == 0, dv_all, dk_all)
    d_kv = (keep.astype(F32) + swap_core(give).astype(F32)).astype(BF16)
    d_kv = sum_scatter(d_kv)
    d_kv = jnp.where(core == 0, rotate(d_kv, cosine, -sine), d_kv).astype(BF16)
    d_query = rotate(d_query_rot.reshape(rows, heads, hd), cosine[:, None], -sine[:, None])
    d_query = d_query.astype(BF16).reshape(rows, heads * hd)
    d_query_all = jnp.concatenate(gather_tp(d_query, core, y), axis=1)
    k0, v0, k1, v1 = gather_tp(d_kv, core, y)
    d_kv_all = jnp.concatenate([k0, k1, v0, v1], axis=1)
    d_normed = mm(d_query_all, q_full, 1, 0) + mm(d_kv_all, kv_weight, 1, 1)
    w_one = inputs * factor_one
    part_attn_gain = jnp.sum(d_normed * w_one, axis=0)
    dg_one = d_normed * gain_one
    dx = d_hidden_in + factor_one * (dg_one - w_one * jnp.mean(dg_one * w_one, axis=-1, keepdims=True))

    gate_t = mm(gate_s, normed_all, 0, 1)
    up_t = mm(up_s, normed_all, 0, 1)
    d_hidden_t = mm(down_s, cot_all, 1, 1)
    sig_t = jax.nn.sigmoid(gate_t)
    hidden_t = (gate_t * sig_t * up_t).astype(BF16)
    d_gate_t = (d_hidden_t * up_t * sig_t * (1.0 + gate_t * (1.0 - sig_t))).astype(BF16)
    d_up_t = (d_hidden_t * gate_t * sig_t).astype(BF16)
    part = width // n
    ff_grads = jnp.concatenate(
        [mm(d_gate_t, normed_all, 1, 0), mm(d_up_t, normed_all, 1, 0), mm(hidden_t, cot_all, 1, 0)], axis=0
    ).astype(BF16)
    ff_grads = ff_grads.reshape(3 * unit, n, part).transpose(1, 0, 2)
    ff_grads = lax.all_to_all(ff_grads, "ctx", split_axis=0, concat_axis=0, tiled=True)
    ff_grads = ff_grads.reshape(n, 3, unit, part).astype(F32)
    g_gate = ff_grads[:, 0].reshape(ff, part).T
    g_up = ff_grads[:, 1].reshape(ff, part).T
    g_down = ff_grads[:, 2].reshape(ff, part)

    g_o = mm(d_attn, attended, 0, 0).astype(BF16)
    g_o = sum_scatter(g_o.reshape(n, part, heads * hd)).T
    g_q = mm(normed, d_query, 0, 0).astype(BF16)
    g_q = sum_scatter(g_q.reshape(n, part, heads * hd))

    small = width // (n * ntp)
    g_kv = mm(normed, d_kv, 0, 0).astype(BF16).reshape(n * ntp, small, hd)
    bias_row = jnp.sum(d_kv.astype(F32), axis=0).astype(BF16)
    bias_rows = jnp.broadcast_to(bias_row[None, None], (n * ntp, EXTRA, hd))
    g_kv = lax.all_to_all(
        jnp.concatenate([g_kv, bias_rows], axis=1), ("ctx", "tp"), split_axis=0, concat_axis=0, tiled=True
    )
    g_kv = jnp.sum(g_kv.reshape(n, ntp, small + EXTRA, hd).astype(F32), axis=0)
    g_kv = jnp.concatenate([g_kv[0], g_kv[2], g_kv[1], g_kv[3]], axis=1)
    bias_size = kv_bias.shape[0] // (n * ntp)
    g_kv_bias = lax.dynamic_slice_in_dim(g_kv[small], (ctx * ntp + tp) * bias_size, bias_size, 0)
    g_kv = g_kv[:small]

    bias_cols = hd // n
    part_q_bias = jnp.sum(d_query.astype(F32), axis=0).reshape(heads, n, bias_cols).transpose(1, 0, 2)
    vectors = jnp.concatenate(
        [part_mlp_gain.reshape(n, part), part_attn_gain.reshape(n, part), part_q_bias.reshape(n, -1)], axis=1
    )
    vectors = sum_scatter(vectors)
    g_mlp_gain = vectors[:part]
    g_attn_gain = vectors[part : 2 * part]
    g_q_bias = vectors[2 * part :].reshape(heads, bias_cols)

    return (
        output,
        dx,
        g_attn_gain,
        g_q,
        g_q_bias,
        g_kv,
        g_kv_bias,
        g_o,
        g_mlp_gain,
        g_gate,
        g_up,
        g_down,
    )


def solution(mesh):
    return jax.shard_map(
        per_device,
        mesh=mesh,
        in_specs=(
            P("ctx", None),
            P("ctx"),
            P("ctx"),
            P(),
            P(None, "tp"),
            P("tp", None),
            P(),
            P(),
            P("tp", None),
            P(),
            P(None, "tp"),
            P(None, "tp"),
            P("tp", None),
            P("ctx", None),
        ),
        out_specs=(
            P("ctx", None),
            P("ctx", None),
            P("ctx"),
            P("ctx", "tp"),
            P("tp", "ctx"),
            P(("ctx", "tp"), None),
            P(("ctx", "tp")),
            P("tp", "ctx"),
            P("ctx"),
            P("ctx", "tp"),
            P("ctx", "tp"),
            P("tp", "ctx"),
        ),
        check_vma=False,
    )
```

```python
import functools

import jax
import jax.numpy as jnp
from jax import lax
from jax.experimental import pallas as pl
from jax.experimental.pallas import tpu as pltpu
from jax.sharding import PartitionSpec as P

RMS_EPS = 1e-06
ROPE_BASE = 1000000.0
LOG2E = 1.4426950408889634
BF16 = jnp.bfloat16
F32 = jnp.float32
EXTRA = 16


def mm(a, b, ca, cb):
    return lax.dot_general(a, b, (((ca,), (cb,)), ((), ())), preferred_element_type=F32)


def rope_tables(positions, head_dim):
    half = head_dim // 2
    freqs = ROPE_BASE ** (-2.0 * jnp.arange(half, dtype=F32) / head_dim)
    angles = positions.astype(F32)[:, None] * freqs[None, :]
    return jnp.cos(angles), jnp.sin(angles)


def rotate(values, cosine, sine):
    half = cosine.shape[-1]
    first, second = values[..., :half], values[..., half:]
    return jnp.concatenate([first * cosine - second * sine, second * cosine + first * sine], axis=-1)


def swap(x, axis):
    return lax.ppermute(x, axis, [(0, 1), (1, 0)])


def gather_tp(x, core, y):
    far = swap(x, "y")
    mate = swap(x, "core")
    far_mate = swap(far, "core")
    a0, a1 = jnp.where(core == 0, x, mate), jnp.where(core == 0, mate, x)
    b0, b1 = jnp.where(core == 0, far, far_mate), jnp.where(core == 0, far_mate, far)
    return [
        jnp.where(y == 0, a0, b0),
        jnp.where(y == 0, a1, b1),
        jnp.where(y == 0, b0, a0),
        jnp.where(y == 0, b1, a1),
    ]


def sum_core(keep, give):
    return (keep + swap(give, "core").astype(F32)).astype(BF16)


def sum_y(half):
    return (half.astype(F32) + swap(half, "y").astype(F32)).astype(BF16)


def join_core(half, core):
    mate = swap(half, "core")
    return jnp.concatenate([jnp.where(core == 0, half, mate), jnp.where(core == 0, mate, half)], axis=0)


def split_core(part, core):
    rows = part.shape[0] // 2
    keep = lax.dynamic_slice_in_dim(part, core * rows, rows, 0)
    return keep, lax.dynamic_slice_in_dim(part, (1 - core) * rows, rows, 0).astype(BF16)


def sum_x(parts, x):
    keep = lax.dynamic_index_in_dim(parts, x, 0, keepdims=False)
    give = lax.dynamic_index_in_dim(parts, 1 - x, 0, keepdims=False)
    return (keep.astype(F32) + swap(give, "x").astype(F32)).astype(BF16)


def along_z(block, distance):
    nz = lax.axis_size("z")
    return lax.ppermute(block, "z", [(i, (i + distance) % nz) for i in range(nz)])


def column_tokens(block, tp):
    quarter = block.shape[0] // 4
    own = lax.dynamic_slice_in_dim(block, tp * quarter, quarter, 0)
    return lax.all_gather(own, ("z", "y", "core"), axis=0, tiled=True)


def column_start(block, tp):
    nz = lax.axis_size("z")
    quarter = block.shape[0] // 4
    own = lax.dynamic_slice_in_dim(block, tp * quarter, quarter, 0)
    return tuple(lax.ppermute(own, "z", [(i, (i + s) % nz) for i in range(nz)]) for s in range(1, nz))


def after(values, *done):
    return lax.optimization_barrier((values, done))[0]


def block_bounds(scal, rows):
    return lax.div(scal[1], rows), scal[0] + 1


def probs_t(scal, kb, qh, lo_row, b, rows, factor, shift, masked):
    s = mm(kb, qh, 1, 1) * factor
    if shift is not None:
        s = s - shift
    p = jnp.exp2(s)
    if masked:
        key = b * rows + lax.broadcasted_iota(jnp.int32, p.shape, 0)
        query = scal[0] * p.shape[1] + lax.broadcasted_iota(jnp.int32, p.shape, 1)
        p = jnp.where((key <= query) & (key >= lo_row), p, 0.0)
    return p


def for_blocks(scal, rows, run):
    start, stop = block_bounds(scal, rows)

    def body(b, carry):
        plain = (b < scal[0]) & (scal[2] <= b * rows)

        @pl.when(plain)
        def _():
            run(b, False)

        @pl.when(jnp.logical_not(plain))
        def _():
            run(b, True)

        return carry

    lax.fori_loop(start, stop, body, 0)


def key_value(scal, refs, b, rows):
    z = lax.div(b, 2)
    near = lax.rem(b, 2) == lax.rem(scal[0], 2)
    mine = jnp.where(near, refs[0][z, 0:rows, :], refs[1][z, 0:rows, :])
    other = jnp.where(near, refs[2][z, 0:rows, :], refs[3][z, 0:rows, :])
    return jnp.where(scal[3] == 0, mine, other), jnp.where(scal[3] == 0, other, mine)


def attend_kernel(scal, q_ref, r0, r1, r2, r3, lo_ref, att_ref, log_ref, acc, tot):
    refs = (r0, r1, r2, r3)
    rows, width = q_ref.shape
    hd = r0.shape[2]
    heads = width // hd
    factor = LOG2E * hd**-0.5
    acc[...] = jnp.zeros_like(acc)
    tot[...] = jnp.zeros_like(tot)

    def run(b, masked):
        kb, vb = key_value(scal, refs, b, rows)
        vt = vb.astype(F32).T.astype(BF16)
        for h in range(heads):
            p = probs_t(
                scal, kb, q_ref[:, h * hd : (h + 1) * hd], lo_ref[...], b, rows, factor, None, masked
            )
            tot[h] += jnp.sum(p.reshape(rows // 8, 8, p.shape[1]), axis=0)
            acc[h] += mm(vt, p.astype(BF16), 1, 0)

    for_blocks(scal, rows, run)
    for h in range(heads):
        total = jnp.sum(tot[h], axis=0, keepdims=True)
        att_ref[:, h * hd : (h + 1) * hd] = (acc[h] / total).T.astype(BF16)
        log_ref[h] = jnp.broadcast_to(jnp.log2(total), log_ref.shape[1:])


def attend_back_kernel(
    scal, q_ref, r0, r1, r2, r3, lo_ref, att_ref, log_ref, d_ref, dq_ref, keep_near, keep_far, give_near, give_far, acc, delta
):
    refs = (r0, r1, r2, r3)
    rows, width = q_ref.shape
    hd = r0.shape[2]
    heads = width // hd
    scale = hd**-0.5
    factor = LOG2E * scale
    acc[...] = jnp.zeros_like(acc)
    for h in range(heads):
        cols = slice(h * hd, (h + 1) * hd)
        both = d_ref[:, cols].astype(F32) * att_ref[:, cols].astype(F32)
        delta[h] = jnp.broadcast_to(jnp.sum(both.T, axis=0, keepdims=True), delta.shape[1:])
    zero = jnp.zeros((rows, hd), BF16)

    def put(b, keep, give):
        nz = keep_near.shape[0]
        z = lax.rem(lax.div(b, 2) - lax.div(scal[0], 2) + nz, nz)
        near = lax.rem(b, 2) == lax.rem(scal[0], 2)

        @pl.when(near)
        def _():
            keep_near[z] = keep
            give_near[z] = give

        @pl.when(jnp.logical_not(near))
        def _():
            keep_far[z] = keep
            give_far[z] = give

    def clear(b, carry):
        put(b, zero, zero)
        return carry

    start, stop = block_bounds(scal, rows)
    lax.fori_loop(0, start, clear, 0)
    lax.fori_loop(stop, 2 * keep_near.shape[0], clear, 0)

    def run(b, masked):
        kb, vb = key_value(scal, refs, b, rows)
        kt = kb.astype(F32).T.astype(BF16)
        dk = jnp.zeros((rows, hd), F32)
        dv = jnp.zeros((rows, hd), F32)
        for h in range(heads):
            cols = slice(h * hd, (h + 1) * hd)
            qh = q_ref[:, cols]
            dh = d_ref[:, cols]
            p = probs_t(scal, kb, qh, lo_ref[...], b, rows, factor, log_ref[h, 0:1, :], masked)
            dp = mm(vb, dh, 1, 1)
            ds = (p * (dp - delta[h, 0:1, :])).astype(BF16)
            dv += mm(p.astype(BF16), dh, 1, 0)
            dk += mm(ds, qh, 1, 0)
            acc[h] += mm(kt, ds, 1, 0)
        dk = (dk * scale).astype(BF16)
        dv = dv.astype(BF16)
        put(b, jnp.where(scal[3] == 0, dk, dv), jnp.where(scal[3] == 0, dv, dk))

    for_blocks(scal, rows, run)
    for h in range(heads):
        dq_ref[:, h * hd : (h + 1) * hd] = (acc[h] * scale).T


VMEM = pl.BlockSpec(memory_space=pltpu.VMEM)
SMEM = pl.BlockSpec(memory_space=pltpu.SMEM)
LIMIT = 56 * 1024 * 1024


def attend(scal, q, kv, lo):
    rows, width = q.shape
    hd = kv[0].shape[2]
    heads = width // hd
    blocks = 2 * kv[0].shape[0]
    work = rows * width * rows * blocks
    return pl.pallas_call(
        attend_kernel,
        in_specs=[SMEM] + [VMEM] * 6,
        out_specs=[VMEM, VMEM],
        out_shape=[
            jax.ShapeDtypeStruct((rows, width), BF16),
            jax.ShapeDtypeStruct((heads, 8, rows), F32),
        ],
        scratch_shapes=[pltpu.VMEM((heads, hd, rows), F32), pltpu.VMEM((heads, 8, rows), F32)],
        compiler_params=pltpu.CompilerParams(vmem_limit_bytes=LIMIT),
        cost_estimate=pl.CostEstimate(
            flops=4 * work, bytes_accessed=16 * kv[0].size, transcendentals=work // hd
        ),
        name="attend",
    )(scal, q, *kv, lo)


def attend_back(scal, q, kv, lo, att, logs, d_att):
    rows, width = q.shape
    hd = kv[0].shape[2]
    heads = width // hd
    blocks = 2 * kv[0].shape[0]
    work = rows * width * rows * blocks
    grads = jax.ShapeDtypeStruct(kv[0].shape[:1] + (rows, hd), BF16)
    return pl.pallas_call(
        attend_back_kernel,
        in_specs=[SMEM] + [VMEM] * 9,
        out_specs=[VMEM] * 5,
        out_shape=[jax.ShapeDtypeStruct((rows, width), F32)] + [grads] * 4,
        scratch_shapes=[pltpu.VMEM((heads, hd, rows), F32), pltpu.VMEM((heads, 8, rows), F32)],
        compiler_params=pltpu.CompilerParams(vmem_limit_bytes=LIMIT),
        cost_estimate=pl.CostEstimate(
            flops=10 * work, bytes_accessed=32 * kv[0].size, transcendentals=work // hd
        ),
        name="attend_back",
    )(scal, q, *kv, lo, att, logs, d_att)


CHUNK = 512


def column_fetch(scal, quarters, nz, quarter, rows, normed, nbuf, nsem, cots=None, cbuf=None, csem=None):
    z, core, y = scal[1], lax.rem(scal[2], 2), lax.div(scal[2], 2)
    per_chunk = CHUNK // quarter
    chunks = [(k, first) for k in range(quarters) for first in range(0, nz, per_chunk)]

    def fetch(c):
        k, first = chunks[c]
        slot = c % nbuf.shape[0]
        q = 2 * ((1 - y) if k % 2 else y) + ((1 - core) if k // 2 else core)
        for i in range(per_chunk):
            dist = first + i
            row = pl.multiple_of(lax.rem(z - dist + nz, nz) * rows + q * quarter, quarter)
            place = pl.ds(i * quarter, quarter)
            pltpu.make_async_copy(normed.at[pl.ds(row, quarter), :], nbuf.at[slot, place, :], nsem.at[slot]).start()
            if cots is None:
                continue
            if dist == 0:
                source = cots[0].at[pl.ds(pl.multiple_of(q * quarter, quarter), quarter), :]
            else:
                source = cots[k + 1].at[pl.ds((dist - 1) * quarter, quarter), :]
            pltpu.make_async_copy(source, cbuf.at[slot, place, :], csem.at[slot]).start()

    for c in range(min(nbuf.shape[0], len(chunks))):
        fetch(c)
    return fetch, len(chunks)


def column_put(scal, acc, keep, give):
    nz, part, _ = keep.shape
    flat = acc[...].T.astype(BF16)
    for i in range(2 * nz):
        value = flat[i * part : (i + 1) * part, :]
        dist = lax.rem(i // 2 - scal[1] + nz, nz)

        @pl.when(scal[0] == i % 2)
        def _(value=value, dist=dist):
            keep[dist] = value

        @pl.when(scal[0] != i % 2)
        def _(value=value, dist=dist):
            give[dist] = value


def column_first_kernel(quarters, scal, normed, *refs):
    cots = refs[: quarters + 1]
    gate_ref, up_ref, down_ref, kd, gd, d_gate_ref, d_up_ref = refs[quarters + 1 : quarters + 8]
    nbuf, cbuf, ad, nsem, csem = refs[quarters + 8 :]
    rows = cots[0].shape[0]
    fetch, count = column_fetch(
        scal, quarters, kd.shape[0], rows // quarters, rows, normed, nbuf, nsem, cots, cbuf, csem
    )
    slots = nbuf.shape[0]
    for c in range(count):
        slot = c % slots
        place = slice(c * CHUNK, (c + 1) * CHUNK)
        pltpu.make_async_copy(nbuf.at[slot], nbuf.at[slot], nsem.at[slot]).wait()
        pltpu.make_async_copy(cbuf.at[slot], cbuf.at[slot], csem.at[slot]).wait()
        gate = mm(gate_ref[...], nbuf[slot], 1, 1)
        up = mm(up_ref[...], nbuf[slot], 1, 1)
        d_hidden = mm(down_ref[...], cbuf[slot], 1, 1)
        sig = 1.0 / (1.0 + jnp.exp(-gate))
        silu = gate * sig
        hidden = (silu * up).astype(BF16)
        d_gate_ref[:, place] = (d_hidden * up * sig * (1.0 + gate * (1.0 - sig))).astype(BF16)
        d_up_ref[:, place] = (d_hidden * silu).astype(BF16)
        grad = mm(hidden, cbuf[slot], 1, 0)
        ad[...] = grad if c == 0 else ad[...] + grad
        if c + slots < count:
            fetch(c + slots)
    column_put(scal, ad, kd, gd)


def column_second_kernel(quarters, rows, scal, normed, d_gate_ref, d_up_ref, kg, gg, ku, gu, nbuf, ag, au, nsem):
    fetch, count = column_fetch(scal, quarters, kg.shape[0], rows // quarters, rows, normed, nbuf, nsem)
    slots = nbuf.shape[0]
    for c in range(count):
        slot = c % slots
        place = slice(c * CHUNK, (c + 1) * CHUNK)
        pltpu.make_async_copy(nbuf.at[slot], nbuf.at[slot], nsem.at[slot]).wait()
        for acc, left in ((ag, d_gate_ref), (au, d_up_ref)):
            grad = mm(left[:, place], nbuf[slot], 1, 0)
            acc[...] = grad if c == 0 else acc[...] + grad
        if c + slots < count:
            fetch(c + slots)
    column_put(scal, ag, kg, gg)
    column_put(scal, au, ku, gu)


ANYWHERE = pl.BlockSpec(memory_space=pl.ANY)


def column_first(scal, normed, cots, gate_s, up_s, down_s, n):
    unit, width = gate_s.shape
    quarters = len(cots) - 1
    tokens = normed.shape[0]
    slots = min(tokens // CHUNK, 4)
    out = jax.ShapeDtypeStruct((n // 2, width // n, unit), BF16)
    units = jax.ShapeDtypeStruct((unit, tokens), BF16)
    return pl.pallas_call(
        functools.partial(column_first_kernel, quarters),
        in_specs=[SMEM] + [ANYWHERE] * (quarters + 2) + [VMEM] * 3,
        out_specs=[VMEM] * 4,
        out_shape=[out] * 2 + [units] * 2,
        scratch_shapes=[pltpu.VMEM((slots, CHUNK, width), BF16)] * 2
        + [pltpu.VMEM((unit, width), F32)]
        + [pltpu.SemaphoreType.DMA((slots,))] * 2,
        compiler_params=pltpu.CompilerParams(vmem_limit_bytes=LIMIT),
        cost_estimate=pl.CostEstimate(
            flops=8 * tokens * width * unit,
            bytes_accessed=4 * tokens * width + 12 * width * unit,
            transcendentals=tokens * unit,
        ),
        name="column_first",
    )(scal, normed, *cots, gate_s, up_s, down_s)


def column_second(scal, normed, d_gate, d_up, rows, n):
    unit, tokens = d_gate.shape
    width = normed.shape[1]
    slots = min(tokens // CHUNK, 4)
    out = jax.ShapeDtypeStruct((n // 2, width // n, unit), BF16)
    return pl.pallas_call(
        functools.partial(column_second_kernel, 4, rows),
        in_specs=[SMEM, ANYWHERE, VMEM, VMEM],
        out_specs=[VMEM] * 4,
        out_shape=[out] * 4,
        scratch_shapes=[pltpu.VMEM((slots, CHUNK, width), BF16)]
        + [pltpu.VMEM((unit, width), F32)] * 2
        + [pltpu.SemaphoreType.DMA((slots,))],
        compiler_params=pltpu.CompilerParams(vmem_limit_bytes=LIMIT),
        cost_estimate=pl.CostEstimate(
            flops=4 * tokens * width * unit,
            bytes_accessed=2 * tokens * width + 4 * width * unit,
            transcendentals=0,
        ),
        name="column_second",
    )(scal, normed, d_gate, d_up)


def assemble_kernel(nz, scal, *refs):
    unit = refs[0].shape[1]
    groups, targets = (refs[:nz], refs[nz : 2 * nz], refs[2 * nz : 3 * nz]), refs[3 * nz :]

    def block(group, j):
        dist = lax.rem(scal[1] - j + nz, nz)
        value = group[0][...]
        for d in range(1, nz):
            value = jnp.where(dist == d, group[d][...], value)
        return value.astype(F32)

    for group, target in zip(groups[:2], targets[:2]):
        target[...] = jnp.concatenate([block(group, j) for j in range(nz)], axis=1)
    for j in range(nz):
        targets[2][j * unit : (j + 1) * unit, :] = block(groups[2], j).T


def assemble(scal, gate, up, down):
    nz = len(gate)
    part, unit = gate[0].shape
    ff = nz * unit
    return pl.pallas_call(
        functools.partial(assemble_kernel, nz),
        in_specs=[SMEM] + [VMEM] * (3 * nz),
        out_specs=[VMEM] * 3,
        out_shape=[jax.ShapeDtypeStruct(shape, F32) for shape in ((part, ff), (part, ff), (ff, part))],
        compiler_params=pltpu.CompilerParams(vmem_limit_bytes=LIMIT),
        cost_estimate=pl.CostEstimate(flops=0, bytes_accessed=18 * ff * part, transcendentals=0),
        name="assemble",
    )(scal, *gate, *up, *down)


def per_device(
    layer_input,
    segment_ids,
    positions,
    attn_gain,
    q_weight,
    q_bias,
    kv_weight,
    kv_bias,
    o_weight,
    mlp_gain,
    gate_weight,
    up_weight,
    down_weight,
    cotangent,
):
    rows, width = layer_input.shape
    heads, hd = q_bias.shape
    ff = gate_weight.shape[1]
    nz, x, y, core = lax.axis_size("z"), lax.axis_index("x"), lax.axis_index("y"), lax.axis_index("core")
    z = lax.axis_index("z")
    n, ntp = 2 * nz, 4
    ctx = 2 * z + x
    tp = 2 * y + core
    unit = ff // nz

    o_full = jnp.concatenate(gather_tp(o_weight, core, y), axis=0)
    gate_s = lax.dynamic_slice_in_dim(gate_weight.T, z * unit, unit, 0)
    up_s = lax.dynamic_slice_in_dim(up_weight.T, z * unit, unit, 0)
    down_s = lax.dynamic_slice_in_dim(down_weight, z * unit, unit, 0)

    inputs = layer_input.astype(F32)
    gain_one = attn_gain.astype(F32)
    factor_one = lax.rsqrt(jnp.mean(inputs * inputs, axis=-1, keepdims=True) + RMS_EPS)
    normed = (inputs * factor_one * gain_one).astype(BF16)
    cosine, sine = rope_tables(positions, hd)
    query = mm(normed, q_weight, 1, 0) + q_bias.astype(F32).reshape(-1)
    query_rot = rotate(query.reshape(rows, heads, hd), cosine[:, None], sine[:, None])
    query_rot = query_rot.astype(BF16).reshape(rows, heads * hd)
    column = (2 * core + y) * hd
    kv_cols = lax.dynamic_slice_in_dim(kv_weight, column, hd, 1)
    kv_own_bias = lax.dynamic_slice_in_dim(kv_bias, column, hd, 0).astype(F32)
    kv_own = mm(normed, kv_cols, 1, 0) + kv_own_bias
    kv_own = jnp.where(core == 0, rotate(kv_own, cosine, sine), kv_own).astype(BF16)

    ids = segment_ids.astype(BF16).reshape(rows // hd, hd)
    ids = jnp.pad(ids, ((0, EXTRA - rows // hd), (0, 0)))
    packed = jnp.concatenate([kv_own, ids], axis=0)
    near = lax.all_to_all(
        jnp.broadcast_to(packed[None], (nz,) + packed.shape), "z", split_axis=0, concat_axis=0, tiled=True
    )
    cot_ahead = column_start(after(cotangent, near), tp)
    far = swap(near, "x")
    kv = (near, far, swap(near, "core"), swap(far, "core"))
    kv, gate_s, up_s, down_s = lax.optimization_barrier((kv, gate_s, up_s, down_s))
    all_ids = jnp.stack([near[:, rows : rows + rows // hd], far[:, rows : rows + rows // hd]]).astype(F32)
    starts = [jnp.sum((all_ids < k).astype(F32)).astype(jnp.int32) for k in (1, 2, 3)]
    lo = jnp.where(
        segment_ids == 0,
        0,
        jnp.where(segment_ids == 1, starts[0], jnp.where(segment_ids == 2, starts[1], starts[2])),
    )
    scal = jnp.stack([ctx, lo[0], lo[-1], core]).astype(jnp.int32)
    lo = lo.reshape(1, rows)

    attended, logs = attend(scal, query_rot, kv, lo)
    attended_all = jnp.concatenate(gather_tp(attended, core, y), axis=1)
    d_hidden = mm(after(cotangent, attended), down_weight, 1, 1).astype(BF16)
    hidden_in = inputs + mm(attended_all, o_full, 1, 0)

    gain_two = mlp_gain.astype(F32)
    factor_two = lax.rsqrt(jnp.mean(hidden_in * hidden_in, axis=-1, keepdims=True) + RMS_EPS)
    normed_two = (hidden_in * factor_two * gain_two).astype(BF16)
    normed_all = column_tokens(normed_two, tp)
    normed_two, cot_ahead = lax.optimization_barrier((normed_two, cot_ahead))

    gate = mm(normed_two, gate_weight, 1, 0)
    up = mm(normed_two, up_weight, 1, 0)
    sig = jax.nn.sigmoid(gate)
    hidden = (gate * sig * up).astype(BF16)
    d_gate = (d_hidden * up * sig * (1.0 + gate * (1.0 - sig))).astype(BF16)
    d_up = (d_hidden * gate * sig).astype(BF16)
    d_normed_two = mm(d_gate, gate_weight, 1, 1) + mm(d_up, up_weight, 1, 1)
    d_half = sum_core(*split_core(d_normed_two, core))
    d_half, hidden = lax.optimization_barrier((d_half, hidden))
    d_half = sum_y(d_half)
    cot_here = jnp.concatenate(after(cot_ahead, d_half), axis=0)
    cot_there = swap(cot_here, "y")
    d_normed_two = join_core(d_half, core).astype(F32)

    w_two = hidden_in * factor_two
    part_mlp_gain = jnp.sum(d_normed_two * w_two, axis=0)
    dg_two = d_normed_two * gain_two
    d_hidden_in = cotangent.astype(F32) + factor_two * (
        dg_two - w_two * jnp.mean(dg_two * w_two, axis=-1, keepdims=True)
    )
    d_attn = d_hidden_in.astype(BF16)
    d_attended = mm(d_attn, o_weight, 1, 1).astype(BF16)
    part = width // n
    g_o = mm(d_attn, attended, 0, 0).astype(BF16).reshape(nz, 2, part, heads * hd).swapaxes(0, 1)
    d_attended, g_o = lax.optimization_barrier((d_attended, g_o))
    g_o = sum_x(g_o, x)

    d_query_rot, keep_near, keep_far, give_near, give_far = attend_back(
        scal, query_rot, kv, lo, attended, logs, d_attended
    )
    d_query_rot, g_o, cot_there = lax.optimization_barrier((d_query_rot, g_o, cot_there))
    cots = (cotangent, cot_here, cot_there, swap(cot_here, "core"), swap(cot_there, "core"))
    d_far = (keep_far.astype(F32) + swap(give_far, "core").astype(F32)).astype(BF16)
    came_near = swap(give_near, "core")
    came_far = swap(d_far, "x")
    g_o = lax.all_to_all(g_o, "z", split_axis=0, concat_axis=0, tiled=True)
    d_query_rot, hidden = after((d_query_rot, hidden), d_far)
    mlp_part = mm(hidden, down_weight, 1, 0)
    o_half = sum_core(*split_core(mlp_part, core))
    d_query = rotate(d_query_rot.reshape(rows, heads, hd), cosine[:, None], -sine[:, None])
    d_query = d_query.astype(BF16).reshape(rows, heads * hd)
    g_q = mm(normed, d_query, 0, 0).astype(BF16).reshape(nz, 2, part, heads * hd).swapaxes(0, 1)
    came_near, g_q, o_half, normed_all, cots = lax.optimization_barrier((came_near, g_q, o_half, normed_all, cots))
    g_q = sum_x(g_q, x)
    o_half = sum_y(o_half)

    place = jnp.stack([x, z, tp]).astype(jnp.int32)
    keep_down, give_down, d_gate_c, d_up_c = column_first(place, normed_all, cots, gate_s, up_s, down_s, n)
    came_far, g_o, g_q, o_half, d_gate_c, d_up_c, give_down = lax.optimization_barrier(
        (came_far, g_o, g_q, o_half, d_gate_c, d_up_c, give_down)
    )
    ring = [
        (keep_near[s].astype(F32) + came_near[s].astype(F32) + came_far[s].astype(F32)).astype(BF16)
        for s in range(nz)
    ]
    ring, give_down, d_gate_c = lax.optimization_barrier((ring, give_down, d_gate_c))
    ring = ring[:1] + [along_z(ring[s], s) for s in range(1, nz)]
    came_down = swap(give_down, "x")
    g_q = lax.all_to_all(g_q, "z", split_axis=0, concat_axis=0, tiled=True)
    keep_gate, give_gate, keep_up, give_up = column_second(place, normed_all, d_gate_c, d_up_c, rows, n)
    came_down, ring, g_q, give_gate, give_up = lax.optimization_barrier((came_down, ring, g_q, give_gate, give_up))
    d_kv = sum(r.astype(F32) for r in ring)
    d_kv = jnp.where(core == 0, rotate(d_kv, cosine, -sine), d_kv).astype(BF16)

    def sum_parts(keep, came):
        return [(keep[s].astype(F32) + came[s].astype(F32)).astype(BF16) for s in range(nz)]

    def spread(sums):
        return sums[:1] + [along_z(sums[s], s) for s in range(1, nz)]

    sums, give_gate = lax.optimization_barrier((sum_parts(keep_down, came_down), give_gate))
    came_gate, g_down = swap(give_gate, "x"), spread(sums)
    d_normed = mm(d_query, q_weight, 1, 1) + mm(d_kv, kv_cols, 1, 1)
    d_normed = sum_core(*split_core(d_normed, core))
    d_normed, came_gate, g_down = lax.optimization_barrier((d_normed, came_gate, g_down))
    sums, give_up = lax.optimization_barrier((sum_parts(keep_gate, came_gate), after(give_up, d_normed)))
    came_up, g_gate = swap(give_up, "x"), spread(sums)
    d_normed = sum_y(d_normed)
    d_normed, came_up, g_gate, o_half = lax.optimization_barrier((d_normed, came_up, g_gate, o_half))
    sums, d_normed = lax.optimization_barrier((sum_parts(keep_up, came_up), d_normed))
    g_up = spread(sums)
    d_normed = join_core(d_normed, core).astype(F32)
    w_one = inputs * factor_one
    part_attn_gain = jnp.sum(d_normed * w_one, axis=0)
    dg_one = d_normed * gain_one
    dx = d_hidden_in + factor_one * (dg_one - w_one * jnp.mean(dg_one * w_one, axis=-1, keepdims=True))
    output = (hidden_in + join_core(o_half, core).astype(F32)).astype(BF16)

    small, bias_cols = width // (n * ntp), hd // n
    g_kv = mm(normed, d_kv, 0, 0).astype(BF16).reshape(nz, 2, ntp, small, hd)
    q_bias_sum = jnp.sum(d_query.astype(F32), axis=0).reshape(heads, n, bias_cols).transpose(1, 0, 2)
    tail_rows = jnp.concatenate(
        [
            jnp.broadcast_to(jnp.sum(d_kv.astype(F32), axis=0), (n, hd)),
            part_mlp_gain.reshape(n, part),
            part_attn_gain.reshape(n, part),
            q_bias_sum.reshape(n, heads * bias_cols),
        ],
        axis=1,
    )
    extra = -(-tail_rows.shape[1] // (EXTRA * hd)) * EXTRA
    tail_rows = jnp.pad(tail_rows, ((0, 0), (0, extra * hd - tail_rows.shape[1]))).astype(BF16)
    tail_rows = jnp.broadcast_to(tail_rows.reshape(nz, 2, 1, extra, hd), (nz, 2, ntp, extra, hd))
    g_kv = sum_x(jnp.concatenate([g_kv, tail_rows], axis=3).swapaxes(0, 1), x)
    g_kv = lax.all_to_all(
        g_kv.reshape(nz * ntp, small + extra, hd), ("z", "y", "core"), split_axis=0, concat_axis=0, tiled=True
    )
    g_kv, dx, output, g_up = lax.optimization_barrier((g_kv, dx, output, g_up))
    g_kv = jnp.sum(g_kv.reshape(nz, ntp, small + extra, hd).astype(F32), axis=0)
    sums = lax.dynamic_index_in_dim(g_kv[:, small:], tp, 0, keepdims=False).reshape(-1)[hd:]
    g_mlp_gain = sums[:part]
    g_attn_gain = sums[part : 2 * part]
    g_q_bias = sums[2 * part : 2 * part + heads * bias_cols].reshape(heads, bias_cols)
    g_kv = jnp.concatenate([g_kv[0], g_kv[2], g_kv[1], g_kv[3]], axis=1)
    bias_size = kv_bias.shape[0] // (n * ntp)
    g_kv_bias = lax.dynamic_slice_in_dim(g_kv[small], (ctx * ntp + tp) * bias_size, bias_size, 0)
    g_kv = g_kv[:small]

    g_gate, g_up, g_down = assemble(place, g_gate, g_up, g_down)
    g_o = jnp.sum(g_o.astype(F32), axis=0).T
    g_q = jnp.sum(g_q.astype(F32), axis=0)

    return (
        output,
        dx,
        g_attn_gain,
        g_q,
        g_q_bias,
        g_kv,
        g_kv_bias,
        g_o,
        g_mlp_gain,
        g_gate,
        g_up,
        g_down,
    )


def solution(mesh):
    n, ntp = mesh.shape["ctx"], mesh.shape["tp"]
    fine = jax.sharding.Mesh(mesh.devices.reshape(n // 2, 2, ntp // 2, 2), ("z", "x", "y", "core"))
    ctx, tp = ("z", "x"), ("y", "core")
    both = ctx + tp
    return jax.shard_map(
        per_device,
        mesh=fine,
        in_specs=(
            P(ctx, None),
            P(ctx),
            P(ctx),
            P(),
            P(None, tp),
            P(tp, None),
            P(),
            P(),
            P(tp, None),
            P(),
            P(None, tp),
            P(None, tp),
            P(tp, None),
            P(ctx, None),
        ),
        out_specs=(
            P(ctx, None),
            P(ctx, None),
            P(ctx),
            P(ctx, tp),
            P(tp, ctx),
            P(both, None),
            P(both),
            P(tp, ctx),
            P(ctx),
            P(ctx, tp),
            P(ctx, tp),
            P(tp, ctx),
        ),
        check_vma=False,
    )
```

```python
import functools

import jax
import jax.numpy as jnp
from jax import lax
from jax.experimental import pallas as pl
from jax.experimental.pallas import tpu as pltpu
from jax.sharding import PartitionSpec as P

RMS_EPS = 1e-06
ROPE_BASE = 1000000.0
LOG2E = 1.4426950408889634
BF16 = jnp.bfloat16
F32 = jnp.float32
EXTRA = 16


def mm(a, b, ca, cb):
    return lax.dot_general(a, b, (((ca,), (cb,)), ((), ())), preferred_element_type=F32)


def rope_tables(positions, head_dim):
    half = head_dim // 2
    freqs = ROPE_BASE ** (-2.0 * jnp.arange(half, dtype=F32) / head_dim)
    angles = positions.astype(F32)[:, None] * freqs[None, :]
    return jnp.cos(angles), jnp.sin(angles)


def rotate(values, cosine, sine):
    half = cosine.shape[-1]
    first, second = values[..., :half], values[..., half:]
    return jnp.concatenate([first * cosine - second * sine, second * cosine + first * sine], axis=-1)


def swap(x, axis):
    return lax.ppermute(x, axis, [(0, 1), (1, 0)])


def gather_tp(x, core, y):
    far = swap(x, "y")
    mate = swap(x, "core")
    far_mate = swap(far, "core")
    a0, a1 = jnp.where(core == 0, x, mate), jnp.where(core == 0, mate, x)
    b0, b1 = jnp.where(core == 0, far, far_mate), jnp.where(core == 0, far_mate, far)
    return [
        jnp.where(y == 0, a0, b0),
        jnp.where(y == 0, a1, b1),
        jnp.where(y == 0, b0, a0),
        jnp.where(y == 0, b1, a1),
    ]


def sum_core(keep, give):
    return (keep + swap(give, "core").astype(F32)).astype(BF16)


def sum_y(half):
    return (half.astype(F32) + swap(half, "y").astype(F32)).astype(BF16)


def join_core(half, core):
    mate = swap(half, "core")
    return jnp.concatenate([jnp.where(core == 0, half, mate), jnp.where(core == 0, mate, half)], axis=0)


def split_core(part, core):
    rows = part.shape[0] // 2
    keep = lax.dynamic_slice_in_dim(part, core * rows, rows, 0)
    return keep, lax.dynamic_slice_in_dim(part, (1 - core) * rows, rows, 0).astype(BF16)


def sum_x(parts, x):
    keep = lax.dynamic_index_in_dim(parts, x, 0, keepdims=False)
    give = lax.dynamic_index_in_dim(parts, 1 - x, 0, keepdims=False)
    return (keep.astype(F32) + swap(give, "x").astype(F32)).astype(BF16)


def along_z(block, distance):
    nz = lax.axis_size("z")
    return lax.ppermute(block, "z", [(i, (i + distance) % nz) for i in range(nz)])


def column_tokens(block, tp):
    quarter = block.shape[0] // 4
    own = lax.dynamic_slice_in_dim(block, tp * quarter, quarter, 0)
    return lax.all_gather(own, ("z", "y", "core"), axis=0, tiled=True)


def after(values, *done):
    return lax.optimization_barrier((values, done))[0]


def block_bounds(scal, rows):
    return lax.div(scal[1], rows), scal[0] + 1


def probs_t(scal, kb, qh, lo_row, b, rows, factor, shift, masked):
    s = mm(kb, qh, 1, 1) * factor
    if shift is not None:
        s = s - shift
    p = jnp.exp2(s)
    if masked:
        key = b * rows + lax.broadcasted_iota(jnp.int32, p.shape, 0)
        query = scal[0] * p.shape[1] + lax.broadcasted_iota(jnp.int32, p.shape, 1)
        p = jnp.where((key <= query) & (key >= lo_row), p, 0.0)
    return p


def for_blocks(scal, rows, run):
    start, stop = block_bounds(scal, rows)

    def body(b, carry):
        plain = (b < scal[0]) & (scal[2] <= b * rows)

        @pl.when(plain)
        def _():
            run(b, False)

        @pl.when(jnp.logical_not(plain))
        def _():
            run(b, True)

        return carry

    lax.fori_loop(start, stop, body, 0)


def key_value(scal, refs, b, rows):
    z = lax.div(b, 2)
    near = lax.rem(b, 2) == lax.rem(scal[0], 2)
    mine = jnp.where(near, refs[0][z, 0:rows, :], refs[1][z, 0:rows, :])
    other = jnp.where(near, refs[2][z, 0:rows, :], refs[3][z, 0:rows, :])
    return jnp.where(scal[3] == 0, mine, other), jnp.where(scal[3] == 0, other, mine)


def attend_kernel(scal, q_ref, r0, r1, r2, r3, lo_ref, att_ref, log_ref, acc, tot):
    refs = (r0, r1, r2, r3)
    rows, width = q_ref.shape
    hd = r0.shape[2]
    heads = width // hd
    factor = LOG2E * hd**-0.5
    acc[...] = jnp.zeros_like(acc)
    tot[...] = jnp.zeros_like(tot)

    def run(b, masked):
        kb, vb = key_value(scal, refs, b, rows)
        vt = vb.astype(F32).T.astype(BF16)
        for h in range(heads):
            p = probs_t(
                scal, kb, q_ref[:, h * hd : (h + 1) * hd], lo_ref[...], b, rows, factor, None, masked
            )
            tot[h] += jnp.sum(p.reshape(rows // 8, 8, p.shape[1]), axis=0)
            acc[h] += mm(vt, p.astype(BF16), 1, 0)

    for_blocks(scal, rows, run)
    for h in range(heads):
        total = jnp.sum(tot[h], axis=0, keepdims=True)
        att_ref[:, h * hd : (h + 1) * hd] = (acc[h] / total).T.astype(BF16)
        log_ref[h] = jnp.broadcast_to(jnp.log2(total), log_ref.shape[1:])


def attend_back_kernel(
    scal, q_ref, r0, r1, r2, r3, lo_ref, att_ref, log_ref, d_ref, cos_ref, sin_ref, dq_ref, keep_near, keep_far, give_near, give_far, acc, delta
):
    refs = (r0, r1, r2, r3)
    rows, width = q_ref.shape
    hd = r0.shape[2]
    heads = width // hd
    scale = hd**-0.5
    factor = LOG2E * scale
    acc[...] = jnp.zeros_like(acc)
    for h in range(heads):
        cols = slice(h * hd, (h + 1) * hd)
        both = d_ref[:, cols].astype(F32) * att_ref[:, cols].astype(F32)
        delta[h] = jnp.broadcast_to(jnp.sum(both.T, axis=0, keepdims=True), delta.shape[1:])
    zero = jnp.zeros((rows, hd), BF16)

    def put(b, keep, give):
        nz = keep_near.shape[0]
        z = lax.rem(lax.div(b, 2) - lax.div(scal[0], 2) + nz, nz)
        near = lax.rem(b, 2) == lax.rem(scal[0], 2)

        @pl.when(near)
        def _():
            keep_near[z] = keep
            give_near[z] = give

        @pl.when(jnp.logical_not(near))
        def _():
            keep_far[z] = keep
            give_far[z] = give

    def clear(b, carry):
        put(b, zero, zero)
        return carry

    start, stop = block_bounds(scal, rows)
    lax.fori_loop(0, start, clear, 0)
    lax.fori_loop(stop, 2 * keep_near.shape[0], clear, 0)

    def run(b, masked):
        kb, vb = key_value(scal, refs, b, rows)
        kt = kb.astype(F32).T.astype(BF16)
        dk = jnp.zeros((rows, hd), F32)
        dv = jnp.zeros((rows, hd), F32)
        for h in range(heads):
            cols = slice(h * hd, (h + 1) * hd)
            qh = q_ref[:, cols]
            dh = d_ref[:, cols]
            p = probs_t(scal, kb, qh, lo_ref[...], b, rows, factor, log_ref[h, 0:1, :], masked)
            dp = mm(vb, dh, 1, 1)
            ds = (p * (dp - delta[h, 0:1, :])).astype(BF16)
            dv += mm(p.astype(BF16), dh, 1, 0)
            dk += mm(ds, qh, 1, 0)
            acc[h] += mm(kt, ds, 1, 0)
        dk = (dk * scale).astype(BF16)
        dv = dv.astype(BF16)
        put(b, jnp.where(scal[3] == 0, dk, dv), jnp.where(scal[3] == 0, dv, dk))

    for_blocks(scal, rows, run)
    for h in range(heads):
        dq = (acc[h] * scale).T
        dq = dq * cos_ref[...] + pltpu.roll(dq, hd // 2, 1) * sin_ref[...]
        dq_ref[:, h * hd : (h + 1) * hd] = dq.astype(BF16)


VMEM = pl.BlockSpec(memory_space=pltpu.VMEM)
SMEM = pl.BlockSpec(memory_space=pltpu.SMEM)
ANYWHERE = pl.BlockSpec(memory_space=pl.ANY)
MIB = 1024 * 1024


def cost(us):
    return pl.CostEstimate(flops=int(us * 1.15e9), bytes_accessed=0, transcendentals=0)


def attend(scal, q, kv, lo):
    rows, width = q.shape
    hd = kv[0].shape[2]
    heads = width // hd
    return pl.pallas_call(
        attend_kernel,
        in_specs=[SMEM] + [VMEM] * 6,
        out_specs=[VMEM, VMEM],
        out_shape=[
            jax.ShapeDtypeStruct((rows, width), BF16),
            jax.ShapeDtypeStruct((heads, 8, rows), F32),
        ],
        scratch_shapes=[pltpu.VMEM((heads, hd, rows), F32), pltpu.VMEM((heads, 8, rows), F32)],
        compiler_params=pltpu.CompilerParams(vmem_limit_bytes=20 * MIB),
        cost_estimate=cost(50),
        name="attend",
    )(scal, q, *kv, lo)


def attend_back(scal, q, kv, lo, att, logs, d_att, cos, sin):
    rows, width = q.shape
    hd = kv[0].shape[2]
    heads = width // hd
    grads = jax.ShapeDtypeStruct(kv[0].shape[:1] + (rows, hd), BF16)
    return pl.pallas_call(
        attend_back_kernel,
        in_specs=[SMEM] + [VMEM] * 11,
        out_specs=[VMEM] * 5,
        out_shape=[jax.ShapeDtypeStruct((rows, width), BF16)] + [grads] * 4,
        scratch_shapes=[pltpu.VMEM((heads, hd, rows), F32), pltpu.VMEM((heads, 8, rows), F32)],
        compiler_params=pltpu.CompilerParams(vmem_limit_bytes=26 * MIB),
        cost_estimate=cost(8),
        name="attend_back",
    )(scal, q, *kv, lo, att, logs, d_att, cos, sin)


CHUNK = 512


def column_fetch(scal, quarters, nz, quarter, rows, normed, nbuf, nsem, cots=None, cbuf=None, csem=None):
    z, core, y = scal[1], lax.rem(scal[2], 2), lax.div(scal[2], 2)
    per_chunk = CHUNK // quarter
    chunks = [(k, first) for k in range(quarters) for first in range(0, nz, per_chunk)]

    def fetch(c):
        k, first = chunks[c]
        slot = c % nbuf.shape[0]
        q = 2 * ((1 - y) if k % 2 else y) + ((1 - core) if k // 2 else core)
        for i in range(per_chunk):
            dist = first + i
            row = pl.multiple_of(lax.rem(z - dist + nz, nz) * rows + q * quarter, quarter)
            place = pl.ds(i * quarter, quarter)
            pltpu.make_async_copy(normed.at[pl.ds(row, quarter), :], nbuf.at[slot, place, :], nsem.at[slot]).start()
            if cots is None:
                continue
            if dist == 0:
                source = cots[0].at[pl.ds(pl.multiple_of(q * quarter, quarter), quarter), :]
            else:
                source = cots[k + 1].at[pl.ds((dist - 1) * quarter, quarter), :]
            pltpu.make_async_copy(source, cbuf.at[slot, place, :], csem.at[slot]).start()

    for c in range(min(nbuf.shape[0], len(chunks))):
        fetch(c)
    return fetch, len(chunks)


def column_put(scal, acc, keep, give):
    nz, part, _ = keep.shape
    flat = acc[...].T.astype(BF16)
    for i in range(2 * nz):
        value = flat[i * part : (i + 1) * part, :]
        dist = lax.rem(i // 2 - scal[1] + nz, nz)

        @pl.when(scal[0] == i % 2)
        def _(value=value, dist=dist):
            keep[dist] = value

        @pl.when(scal[0] != i % 2)
        def _(value=value, dist=dist):
            give[dist] = value


def column_first_kernel(quarters, scal, normed, *refs):
    cots = refs[: quarters + 1]
    gate_ref, up_ref, down_ref, kd, gd, d_gate_ref, d_up_ref = refs[quarters + 1 : quarters + 8]
    nbuf, cbuf, ad, nsem, csem = refs[quarters + 8 :]
    rows = cots[0].shape[0]
    fetch, count = column_fetch(
        scal, quarters, kd.shape[0], rows // quarters, rows, normed, nbuf, nsem, cots, cbuf, csem
    )
    slots = nbuf.shape[0]
    for c in range(count):
        slot = c % slots
        place = slice(c * CHUNK, (c + 1) * CHUNK)
        pltpu.make_async_copy(nbuf.at[slot], nbuf.at[slot], nsem.at[slot]).wait()
        pltpu.make_async_copy(cbuf.at[slot], cbuf.at[slot], csem.at[slot]).wait()
        gate = mm(gate_ref[...], nbuf[slot], 1, 1)
        up = mm(up_ref[...], nbuf[slot], 1, 1)
        d_hidden = mm(down_ref[...], cbuf[slot], 1, 1)
        sig = 1.0 / (1.0 + jnp.exp(-gate))
        silu = gate * sig
        hidden = (silu * up).astype(BF16)
        d_gate_ref[:, place] = (d_hidden * up * sig * (1.0 + gate * (1.0 - sig))).astype(BF16)
        d_up_ref[:, place] = (d_hidden * silu).astype(BF16)
        grad = mm(hidden, cbuf[slot], 1, 0)
        ad[...] = grad if c == 0 else ad[...] + grad
        if c + slots < count:
            fetch(c + slots)
    column_put(scal, ad, kd, gd)


def column_second_kernel(quarters, rows, scal, normed, d_gate_ref, d_up_ref, kg, gg, ku, gu, nbuf, ag, au, nsem):
    fetch, count = column_fetch(scal, quarters, kg.shape[0], rows // quarters, rows, normed, nbuf, nsem)
    slots = nbuf.shape[0]
    for c in range(count):
        slot = c % slots
        place = slice(c * CHUNK, (c + 1) * CHUNK)
        pltpu.make_async_copy(nbuf.at[slot], nbuf.at[slot], nsem.at[slot]).wait()
        for acc, left in ((ag, d_gate_ref), (au, d_up_ref)):
            grad = mm(left[:, place], nbuf[slot], 1, 0)
            acc[...] = grad if c == 0 else acc[...] + grad
        if c + slots < count:
            fetch(c + slots)
    column_put(scal, ag, kg, gg)
    column_put(scal, au, ku, gu)


def column_first(scal, normed, cots, gate_s, up_s, down_s, n):
    unit, width = gate_s.shape
    quarters = len(cots) - 1
    tokens = normed.shape[0]
    slots = min(tokens // CHUNK, 4)
    out = jax.ShapeDtypeStruct((n // 2, width // n, unit), BF16)
    units = jax.ShapeDtypeStruct((unit, tokens), BF16)
    return pl.pallas_call(
        functools.partial(column_first_kernel, quarters),
        in_specs=[SMEM] + [ANYWHERE] * (quarters + 2) + [VMEM] * 3,
        out_specs=[VMEM] * 4,
        out_shape=[out] * 2 + [units] * 2,
        scratch_shapes=[pltpu.VMEM((slots, CHUNK, width), BF16)] * 2
        + [pltpu.VMEM((unit, width), F32)]
        + [pltpu.SemaphoreType.DMA((slots,))] * 2,
        compiler_params=pltpu.CompilerParams(vmem_limit_bytes=50 * MIB),
        cost_estimate=cost(14),
        name="column_first",
    )(scal, normed, *cots, gate_s, up_s, down_s)


def column_second(scal, normed, d_gate, d_up, rows, n):
    unit, tokens = d_gate.shape
    width = normed.shape[1]
    slots = min(tokens // CHUNK, 4)
    out = jax.ShapeDtypeStruct((n // 2, width // n, unit), BF16)
    return pl.pallas_call(
        functools.partial(column_second_kernel, 4, rows),
        in_specs=[SMEM, ANYWHERE, VMEM, VMEM],
        out_specs=[VMEM] * 4,
        out_shape=[out] * 4,
        scratch_shapes=[pltpu.VMEM((slots, CHUNK, width), BF16)]
        + [pltpu.VMEM((unit, width), F32)] * 2
        + [pltpu.SemaphoreType.DMA((slots,))],
        compiler_params=pltpu.CompilerParams(vmem_limit_bytes=40 * MIB),
        cost_estimate=cost(10),
        name="column_second",
    )(scal, normed, d_gate, d_up)


FF_STEPS = 4


def mlp_kernel(scal, n_ref, dh_ref, gate_ref, up_ref, hidden_ref, d_keep, d_give, d_acc):
    step = pl.program_id(0)
    gate = mm(gate_ref[...], n_ref[...], 1, 1)
    up = mm(up_ref[...], n_ref[...], 1, 1)
    d_hidden = dh_ref[...].astype(F32)
    sig = 1.0 / (1.0 + jnp.exp(-gate))
    silu = gate * sig
    hidden_ref[...] = (silu * up).astype(BF16)
    d_gate = (d_hidden * up * sig * (1.0 + gate * (1.0 - sig))).astype(BF16)
    d_up = (d_hidden * silu).astype(BF16)
    d_normed = mm(d_gate, gate_ref[...], 0, 0) + mm(d_up, up_ref[...], 0, 0)

    @pl.when(step == 0)
    def _():
        d_acc[...] = d_normed

    @pl.when(step > 0)
    def _():
        d_acc[...] += d_normed

    @pl.when(step == FF_STEPS - 1)
    def _():
        halves(scal[0], d_acc, d_keep, d_give)


def mlp(core, normed, d_hidden, gate_t, up_t):
    rows, width = normed.shape
    ff = gate_t.shape[0]
    units = pl.BlockSpec((ff // FF_STEPS, width), lambda i: (i, 0))
    tokens = pl.BlockSpec((ff // FF_STEPS, rows), lambda i: (i, 0))
    return pl.pallas_call(
        mlp_kernel,
        grid=(FF_STEPS,),
        in_specs=[SMEM, VMEM, tokens, units, units],
        out_specs=[tokens, VMEM, VMEM],
        out_shape=[
            jax.ShapeDtypeStruct((ff, rows), BF16),
            jax.ShapeDtypeStruct((rows // 2, width), F32),
            jax.ShapeDtypeStruct((rows // 2, width), BF16),
        ],
        scratch_shapes=[pltpu.VMEM((rows, width), F32)],
        compiler_params=pltpu.CompilerParams(vmem_limit_bytes=40 * MIB, dimension_semantics=("arbitrary",)),
        cost_estimate=cost(12),
        name="mlp",
    )(core.reshape(1).astype(jnp.int32), normed, d_hidden, gate_t, up_t)


def halves(core, total, keep, give):
    half = total.shape[0] // 2
    keep[...] = total[pl.ds(pl.multiple_of(core * half, half), half), :]
    give[...] = total[pl.ds(pl.multiple_of((1 - core) * half, half), half), :].astype(BF16)


def project_kernel(scal, *refs):
    count = len(refs) - 13
    ring, (cos_ref, sin_ref, q_ref, qw_ref, kvw_ref, h_ref, down_ref) = refs[:count], refs[count : count + 7]
    kv_ref, d_keep, d_give, o_keep, o_give, total = refs[count + 7 :]
    d_kv = ring[0][...].astype(F32)
    for piece in ring[1:]:
        d_kv += piece[...].astype(F32)
    turned = d_kv * cos_ref[...] + pltpu.roll(d_kv, d_kv.shape[1] // 2, 1) * sin_ref[...]
    d_kv = jnp.where(scal[0] == 0, turned, d_kv).astype(BF16)
    kv_ref[...] = d_kv
    total[...] = mm(q_ref[...], qw_ref[...], 1, 1) + mm(d_kv, kvw_ref[...], 1, 1)
    halves(scal[0], total, d_keep, d_give)
    total[...] = mm(h_ref[...], down_ref[...], 0, 0)
    halves(scal[0], total, o_keep, o_give)


def project(core, ring, cos, sin, d_query, q_weight, kv_cols, hidden, down):
    rows, width = d_query.shape[0], q_weight.shape[0]
    keep = jax.ShapeDtypeStruct((rows // 2, width), F32)
    give = jax.ShapeDtypeStruct((rows // 2, width), BF16)
    return pl.pallas_call(
        project_kernel,
        in_specs=[SMEM] + [VMEM] * (len(ring) + 7),
        out_specs=[VMEM] * 5,
        out_shape=[jax.ShapeDtypeStruct(ring[0].shape, BF16), keep, give, keep, give],
        scratch_shapes=[pltpu.VMEM((rows, width), F32)],
        compiler_params=pltpu.CompilerParams(vmem_limit_bytes=36 * MIB),
        cost_estimate=cost(30),
        name="project",
    )(core.reshape(1).astype(jnp.int32), *ring, cos, sin, d_query, q_weight, kv_cols, hidden, down)


def norm_back_kernel(x_ref, factor_ref, gain_ref, dn_ref, base_ref, dx_ref, gain_grad_ref):
    factor = factor_ref[...]
    w = x_ref[...].astype(F32) * factor
    dn = dn_ref[...].astype(F32)
    gain_grad_ref[...] = jnp.sum(dn * w, axis=0, keepdims=True)
    dg = dn * gain_ref[...].astype(F32)
    dx_ref[...] = base_ref[...] + factor * (dg - w * jnp.mean(dg * w, axis=-1, keepdims=True))


def norm_back(x, factor, gain, dn, base):
    rows, width = x.shape
    return pl.pallas_call(
        norm_back_kernel,
        in_specs=[VMEM] * 5,
        out_specs=[VMEM] * 2,
        out_shape=[jax.ShapeDtypeStruct((rows, width), F32), jax.ShapeDtypeStruct((1, width), F32)],
        compiler_params=pltpu.CompilerParams(vmem_limit_bytes=24 * MIB),
        cost_estimate=cost(30),
        name="norm_back",
    )(x, factor, gain.reshape(1, width), dn, base)


def assemble_kernel(nz, scal, *refs):
    unit = refs[0].shape[1]
    groups, targets = (refs[:nz], refs[nz : 2 * nz], refs[2 * nz : 3 * nz]), refs[3 * nz :]

    def block(group, j):
        dist = lax.rem(scal[1] - j + nz, nz)
        value = group[0][...]
        for d in range(1, nz):
            value = jnp.where(dist == d, group[d][...], value)
        return value.astype(F32)

    for group, target in zip(groups, targets):
        target[...] = jnp.concatenate([block(group, j) for j in range(nz)], axis=1)


def assemble(scal, gate, up, down):
    nz = len(gate)
    part, unit = gate[0].shape
    ff = nz * unit
    return pl.pallas_call(
        functools.partial(assemble_kernel, nz),
        in_specs=[SMEM] + [VMEM] * (3 * nz),
        out_specs=[VMEM] * 3,
        out_shape=[jax.ShapeDtypeStruct((part, ff), F32)] * 3,
        compiler_params=pltpu.CompilerParams(vmem_limit_bytes=28 * MIB),
        cost_estimate=cost(5),
        name="assemble",
    )(scal, *gate, *up, *down)


def per_device(
    layer_input,
    segment_ids,
    positions,
    attn_gain,
    q_weight,
    q_bias,
    kv_weight,
    kv_bias,
    o_weight,
    mlp_gain,
    gate_weight,
    up_weight,
    down_weight,
    cotangent,
):
    rows, width = layer_input.shape
    heads, hd = q_bias.shape
    ff = gate_weight.shape[1]
    nz, x, y, core = lax.axis_size("z"), lax.axis_index("x"), lax.axis_index("y"), lax.axis_index("core")
    z = lax.axis_index("z")
    n, ntp = 2 * nz, 4
    ctx = 2 * z + x
    tp = 2 * y + core
    unit = ff // nz

    o_full = jnp.concatenate(gather_tp(o_weight, core, y), axis=0)
    gate_s = lax.dynamic_slice_in_dim(gate_weight.T, z * unit, unit, 0)
    up_s = lax.dynamic_slice_in_dim(up_weight.T, z * unit, unit, 0)
    down_s = lax.dynamic_slice_in_dim(down_weight, z * unit, unit, 0)

    inputs = layer_input.astype(F32)
    gain_one = attn_gain.astype(F32)
    factor_one = lax.rsqrt(jnp.mean(inputs * inputs, axis=-1, keepdims=True) + RMS_EPS)
    normed = (inputs * factor_one * gain_one).astype(BF16)
    cosine, sine = rope_tables(positions, hd)
    cos_back = jnp.concatenate([cosine, cosine], axis=1)
    sin_back = jnp.concatenate([sine, -sine], axis=1)
    query = mm(normed, q_weight, 1, 0) + q_bias.astype(F32).reshape(-1)
    query_rot = rotate(query.reshape(rows, heads, hd), cosine[:, None], sine[:, None])
    query_rot = query_rot.astype(BF16).reshape(rows, heads * hd)
    column = (2 * core + y) * hd
    kv_cols = lax.dynamic_slice_in_dim(kv_weight, column, hd, 1)
    kv_own_bias = lax.dynamic_slice_in_dim(kv_bias, column, hd, 0).astype(F32)
    kv_own = mm(normed, kv_cols, 1, 0) + kv_own_bias
    kv_own = jnp.where(core == 0, rotate(kv_own, cosine, sine), kv_own).astype(BF16)

    ids = segment_ids.astype(BF16).reshape(rows // hd, hd)
    ids = jnp.pad(ids, ((0, EXTRA - rows // hd), (0, 0)))
    packed = jnp.concatenate([kv_own, ids], axis=0)
    near = lax.all_to_all(
        jnp.broadcast_to(packed[None], (nz,) + packed.shape), "z", split_axis=0, concat_axis=0, tiled=True
    )
    quarter = rows // ntp
    cot_own = lax.dynamic_slice_in_dim(after(cotangent, near), tp * quarter, quarter, 0)
    cot_ahead = [along_z(cot_own, 1)]
    far = swap(near, "x")
    kv = (near, far, swap(near, "core"), swap(far, "core"))
    kv, gate_s, up_s, down_s = lax.optimization_barrier((kv, gate_s, up_s, down_s))
    all_ids = jnp.stack([near[:, rows : rows + rows // hd], far[:, rows : rows + rows // hd]]).astype(F32)
    starts = [jnp.sum((all_ids < k).astype(F32)).astype(jnp.int32) for k in (1, 2, 3)]
    lo = jnp.where(
        segment_ids == 0,
        0,
        jnp.where(segment_ids == 1, starts[0], jnp.where(segment_ids == 2, starts[1], starts[2])),
    )
    scal = jnp.stack([ctx, lo[0], lo[-1], core]).astype(jnp.int32)
    lo = lo.reshape(1, rows)

    attended, logs = attend(scal, query_rot, kv, lo)
    attended, logs, cot_ahead = lax.optimization_barrier((attended, logs, cot_ahead))
    cot_ahead += [along_z(cot_ahead[-1], 1)]
    d_hidden = mm(down_weight, after(cotangent, attended), 1, 1).astype(BF16)
    attended_all = jnp.concatenate(gather_tp(attended, core, y), axis=1)
    attended_all, d_hidden, cot_ahead = lax.optimization_barrier((attended_all, d_hidden, cot_ahead))
    while len(cot_ahead) < nz - 1:
        cot_ahead += [along_z(cot_ahead[-1], 1)]
    hidden_in = inputs + mm(attended_all, o_full, 1, 0)

    gain_two = mlp_gain.astype(F32)
    factor_two = lax.rsqrt(jnp.mean(hidden_in * hidden_in, axis=-1, keepdims=True) + RMS_EPS)
    normed_two = (hidden_in * factor_two * gain_two).astype(BF16)
    normed_all = column_tokens(normed_two, tp)

    hidden, d_keep, d_give = mlp(core, normed_two, d_hidden, gate_weight.T, up_weight.T)
    hidden, d_keep, d_give, cot_ahead = lax.optimization_barrier((hidden, d_keep, d_give, cot_ahead))
    d_half = sum_y(sum_core(d_keep, d_give))
    cot_here = jnp.concatenate(after(cot_ahead, d_half), axis=0)
    cot_there = swap(cot_here, "y")
    d_normed_two = join_core(d_half, core).astype(F32)

    w_two = hidden_in * factor_two
    part_mlp_gain = jnp.sum(d_normed_two * w_two, axis=0)
    dg_two = d_normed_two * gain_two
    d_hidden_in = cotangent.astype(F32) + factor_two * (
        dg_two - w_two * jnp.mean(dg_two * w_two, axis=-1, keepdims=True)
    )
    d_attn = d_hidden_in.astype(BF16)
    d_attended = mm(d_attn, o_weight, 1, 1).astype(BF16)
    part, small = width // n, width // (n * ntp)
    g_o = mm(d_attn, attended, 0, 0).astype(BF16).reshape(nz, 2, part, heads * hd).swapaxes(0, 1)
    keep_o = lax.dynamic_index_in_dim(g_o, x, 0, keepdims=False)
    give_o = lax.dynamic_index_in_dim(g_o, 1 - x, 0, keepdims=False)
    d_attended, keep_o, give_o = lax.optimization_barrier((d_attended, keep_o, give_o))
    came_o = swap(give_o, "x")

    back = attend_back(scal, query_rot, kv, lo, attended, logs, d_attended, cos_back, sin_back)
    back, came_o, cot_there = lax.optimization_barrier((back, came_o, cot_there))
    d_query, keep_near, keep_far, give_near, give_far = back
    cots = (cotangent, cot_here, cot_there, swap(cot_here, "core"), swap(cot_there, "core"))
    d_far = (keep_far.astype(F32) + swap(give_far, "core").astype(F32)).astype(BF16)
    came_near = swap(give_near, "core")
    g_q = mm(normed, after(d_query, d_far), 0, 0).astype(BF16).reshape(nz, 2, part, heads * hd)
    keep_q = lax.dynamic_index_in_dim(g_q, x, 1, keepdims=False)
    give_q = lax.dynamic_index_in_dim(g_q, 1 - x, 1, keepdims=False)
    came_near, d_far, keep_q, give_q, normed_all, cots = lax.optimization_barrier(
        (came_near, d_far, keep_q, give_q, normed_all, cots)
    )
    came_far, came_q = swap(d_far, "x"), swap(give_q, "x")

    place = jnp.stack([x, z, tp]).astype(jnp.int32)
    keep_down, give_down, d_gate_c, d_up_c = column_first(place, normed_all, cots, gate_s, up_s, down_s, n)
    came_far, came_q, d_gate_c, give_down = lax.optimization_barrier((came_far, came_q, d_gate_c, give_down))
    ring = [
        (keep_near[s].astype(F32) + came_near[s].astype(F32) + came_far[s].astype(F32)).astype(BF16)
        for s in range(nz)
    ]
    ring, give_down, d_gate_c = lax.optimization_barrier((ring, give_down, d_gate_c))
    ring = ring[:1] + [along_z(ring[s], s) for s in range(1, nz)]
    came_down = swap(give_down, "x")
    keep_gate, give_gate, keep_up, give_up = column_second(place, normed_all, d_gate_c, d_up_c, rows, n)
    came_down, ring, give_gate, give_up = lax.optimization_barrier((came_down, ring, give_gate, give_up))

    def sum_parts(keep, came):
        return [(keep[s].astype(F32) + came[s].astype(F32)).astype(BF16) for s in range(nz)]

    def spread(sums):
        return sums[:1] + [along_z(sums[s], s) for s in range(1, nz)]

    sums, give_gate, ring = lax.optimization_barrier((sum_parts(keep_down, came_down), give_gate, ring))
    came_gate, g_down = swap(give_gate, "x"), spread(sums)
    parts = project(core, ring, cos_back, sin_back, d_query, q_weight, kv_cols, hidden, down_weight)
    parts, came_gate, g_down = lax.optimization_barrier((parts, came_gate, g_down))
    d_kv = parts[0]
    sums, give_up, parts = lax.optimization_barrier((sum_parts(keep_gate, came_gate), give_up, parts))
    came_up, g_gate = swap(give_up, "x"), spread(sums)
    d_normed = sum_y(sum_core(*parts[1:3]))
    o_half = sum_core(*parts[3:])
    g_o = (keep_o.astype(F32) + came_o.astype(F32)).astype(BF16)
    g_q = (keep_q.astype(F32) + came_q.astype(F32)).astype(BF16)
    g_oq = jnp.concatenate([g_o, g_q], axis=2)
    g_oq = [lax.dynamic_index_in_dim(g_oq, lax.rem(z + s, nz), 0, keepdims=False) for s in range(nz)]
    g_kv = mm(normed, d_kv, 0, 0).astype(BF16).reshape(n * ntp, small, hd)
    d_normed, came_up, g_gate, o_half, g_oq, g_kv = lax.optimization_barrier(
        (d_normed, came_up, g_gate, o_half, g_oq, g_kv)
    )
    sums, d_normed = lax.optimization_barrier((sum_parts(keep_up, came_up), d_normed))
    g_up = spread(sums)
    g_oq = spread(g_oq)
    o_half = sum_y(o_half)
    d_normed = join_core(d_normed, core)
    dx, part_attn_gain = norm_back(layer_input, factor_one, attn_gain, d_normed, d_hidden_in)
    dx, part_attn_gain, g_up, o_half = lax.optimization_barrier((dx, part_attn_gain, g_up, o_half))
    output = (hidden_in + join_core(o_half, core).astype(F32)).astype(BF16)

    bias_cols = hd // n
    q_bias_sum = jnp.sum(d_query.astype(F32), axis=0).reshape(heads, n, bias_cols).transpose(1, 0, 2)
    tail_rows = jnp.concatenate(
        [
            jnp.broadcast_to(jnp.sum(d_kv.astype(F32), axis=0), (n, hd)),
            part_mlp_gain.reshape(n, part),
            part_attn_gain.reshape(n, part),
            q_bias_sum.reshape(n, heads * bias_cols),
        ],
        axis=1,
    )
    extra = -(-tail_rows.shape[1] // (EXTRA * hd)) * EXTRA
    tail_rows = jnp.pad(tail_rows, ((0, 0), (0, extra * hd - tail_rows.shape[1]))).astype(BF16)
    tail_rows = jnp.broadcast_to(tail_rows.reshape(n, 1, extra, hd), (n, ntp, extra, hd)).reshape(-1, extra, hd)
    g_kv = lax.all_to_all(
        jnp.concatenate([g_kv, tail_rows], axis=1), ("z", "x", "y", "core"), split_axis=0, concat_axis=0, tiled=True
    )
    g_kv, dx, output, g_oq = lax.optimization_barrier((g_kv, dx, output, g_oq))
    g_kv = jnp.sum(g_kv.reshape(n, ntp, small + extra, hd).astype(F32), axis=0)
    sums = lax.dynamic_index_in_dim(g_kv[:, small:], tp, 0, keepdims=False).reshape(-1)[hd:]
    g_mlp_gain = sums[:part]
    g_attn_gain = sums[part : 2 * part]
    g_q_bias = sums[2 * part : 2 * part + heads * bias_cols].reshape(heads, bias_cols)
    g_kv = jnp.concatenate([g_kv[0], g_kv[2], g_kv[1], g_kv[3]], axis=1)
    bias_size = kv_bias.shape[0] // (n * ntp)
    g_kv_bias = lax.dynamic_slice_in_dim(g_kv[small], (ctx * ntp + tp) * bias_size, bias_size, 0)
    g_kv = g_kv[:small]

    g_gate, g_up, g_down = assemble(place, g_gate, g_up, g_down)
    g_down = g_down.T
    g_oq = sum(g.astype(F32) for g in g_oq)
    g_o, g_q = g_oq[:, : heads * hd].T, g_oq[:, heads * hd :]

    return (
        output,
        dx,
        g_attn_gain,
        g_q,
        g_q_bias,
        g_kv,
        g_kv_bias,
        g_o,
        g_mlp_gain,
        g_gate,
        g_up,
        g_down,
    )


def solution(mesh):
    n, ntp = mesh.shape["ctx"], mesh.shape["tp"]
    fine = jax.sharding.Mesh(mesh.devices.reshape(n // 2, 2, ntp // 2, 2), ("z", "x", "y", "core"))
    ctx, tp = ("z", "x"), ("y", "core")
    both = ctx + tp
    return jax.shard_map(
        per_device,
        mesh=fine,
        in_specs=(
            P(ctx, None),
            P(ctx),
            P(ctx),
            P(),
            P(None, tp),
            P(tp, None),
            P(),
            P(),
            P(tp, None),
            P(),
            P(None, tp),
            P(None, tp),
            P(tp, None),
            P(ctx, None),
        ),
        out_specs=(
            P(ctx, None),
            P(ctx, None),
            P(ctx),
            P(ctx, tp),
            P(tp, ctx),
            P(both, None),
            P(both),
            P(tp, ctx),
            P(ctx),
            P(ctx, tp),
            P(ctx, tp),
            P(tp, ctx),
        ),
        check_vma=False,
    )
```

```python
import functools

import jax
import jax.numpy as jnp
from jax import lax
from jax.experimental import pallas as pl
from jax.experimental.pallas import tpu as pltpu
from jax.sharding import PartitionSpec as P

RMS_EPS = 1e-06
ROPE_BASE = 1000000.0
LOG2E = 1.4426950408889634
BF16 = jnp.bfloat16
F32 = jnp.float32
EXTRA = 16


def mm(a, b, ca, cb):
    return lax.dot_general(a, b, (((ca,), (cb,)), ((), ())), preferred_element_type=F32)


def rope_tables(positions, head_dim):
    half = head_dim // 2
    freqs = ROPE_BASE ** (-2.0 * jnp.arange(half, dtype=F32) / head_dim)
    angles = positions.astype(F32)[:, None] * freqs[None, :]
    return jnp.cos(angles), jnp.sin(angles)


def rotate(values, cosine, sine):
    half = cosine.shape[-1]
    first, second = values[..., :half], values[..., half:]
    return jnp.concatenate([first * cosine - second * sine, second * cosine + first * sine], axis=-1)


def swap(x, axis):
    return lax.ppermute(x, axis, [(0, 1), (1, 0)])


def gather_tp(x, core, y):
    far = swap(x, "y")
    mate = swap(x, "core")
    far_mate = swap(far, "core")
    a0, a1 = jnp.where(core == 0, x, mate), jnp.where(core == 0, mate, x)
    b0, b1 = jnp.where(core == 0, far, far_mate), jnp.where(core == 0, far_mate, far)
    return [
        jnp.where(y == 0, a0, b0),
        jnp.where(y == 0, a1, b1),
        jnp.where(y == 0, b0, a0),
        jnp.where(y == 0, b1, a1),
    ]


def sum_core(keep, give):
    return (keep + swap(give, "core").astype(F32)).astype(BF16)


def sum_y(half):
    return (half.astype(F32) + swap(half, "y").astype(F32)).astype(BF16)


def join_core(half, core):
    mate = swap(half, "core")
    return jnp.concatenate([jnp.where(core == 0, half, mate), jnp.where(core == 0, mate, half)], axis=0)


def split_core(part, core):
    rows = part.shape[0] // 2
    keep = lax.dynamic_slice_in_dim(part, core * rows, rows, 0)
    return keep, lax.dynamic_slice_in_dim(part, (1 - core) * rows, rows, 0).astype(BF16)


def sum_x(parts, x):
    keep = lax.dynamic_index_in_dim(parts, x, 0, keepdims=False)
    give = lax.dynamic_index_in_dim(parts, 1 - x, 0, keepdims=False)
    return (keep.astype(F32) + swap(give, "x").astype(F32)).astype(BF16)


def by_distance(parts, z):
    nz = parts.shape[0]
    return [lax.dynamic_index_in_dim(parts, lax.rem(z + s, nz), 0, keepdims=False) for s in range(nz)]


def sum_parts(keep, came):
    return [(keep[s].astype(F32) + came[s].astype(F32)).astype(BF16) for s in range(keep.shape[0])]


def spread(sums):
    return sums[:1] + [along_z(sums[s], s) for s in range(1, len(sums))]


def along_z(block, distance):
    nz = lax.axis_size("z")
    return lax.ppermute(block, "z", [(i, (i + distance) % nz) for i in range(nz)])


def column_tokens(block, core):
    half = block.shape[0] // 2
    own = lax.dynamic_slice_in_dim(block, core * half, half, 0)
    return lax.all_gather(own, ("z", "core"), axis=0, tiled=True)


def after(values, *done):
    return lax.optimization_barrier((values, done))[0]


def block_bounds(scal, rows):
    return lax.div(scal[1], rows), scal[0] + 1


def probs_t(scal, kb, qh, lo_row, b, rows, factor, shift, masked):
    s = mm(kb, qh, 1, 1) * factor
    if shift is not None:
        s = s - shift
    p = jnp.exp2(s)
    if masked:
        key = b * rows + lax.broadcasted_iota(jnp.int32, p.shape, 0)
        query = scal[0] * p.shape[1] + lax.broadcasted_iota(jnp.int32, p.shape, 1)
        p = jnp.where((key <= query) & (key >= lo_row), p, 0.0)
    return p


def for_blocks(scal, rows, run):
    start, stop = block_bounds(scal, rows)

    def body(b, carry):
        plain = (b < scal[0]) & (scal[2] <= b * rows)

        @pl.when(plain)
        def _():
            run(b, False)

        @pl.when(jnp.logical_not(plain))
        def _():
            run(b, True)

        return carry

    lax.fori_loop(start, stop, body, 0)


def key_value(scal, refs, b, rows):
    z = lax.div(b, 2)
    near = lax.rem(b, 2) == lax.rem(scal[0], 2)
    mine = jnp.where(near, refs[0][z, 0:rows, :], refs[1][z, 0:rows, :])
    other = jnp.where(near, refs[2][z, 0:rows, :], refs[3][z, 0:rows, :])
    return jnp.where(scal[3] == 0, mine, other), jnp.where(scal[3] == 0, other, mine)


def attend_kernel(scal, q_ref, r0, r1, r2, r3, lo_ref, att_ref, log_ref, acc, tot):
    refs = (r0, r1, r2, r3)
    rows, width = q_ref.shape
    hd = r0.shape[2]
    heads = width // hd
    factor = LOG2E * hd**-0.5
    acc[...] = jnp.zeros_like(acc)
    tot[...] = jnp.zeros_like(tot)

    def run(b, masked):
        kb, vb = key_value(scal, refs, b, rows)
        vt = vb.astype(F32).T.astype(BF16)
        for h in range(heads):
            p = probs_t(
                scal, kb, q_ref[:, h * hd : (h + 1) * hd], lo_ref[...], b, rows, factor, None, masked
            )
            tot[h] += jnp.sum(p.reshape(rows // 8, 8, p.shape[1]), axis=0)
            acc[h] += mm(vt, p.astype(BF16), 1, 0)

    for_blocks(scal, rows, run)
    for h in range(heads):
        total = jnp.sum(tot[h], axis=0, keepdims=True)
        att_ref[:, h * hd : (h + 1) * hd] = (acc[h] / total).T.astype(BF16)
        log_ref[h] = jnp.broadcast_to(jnp.log2(total), log_ref.shape[1:])


def attend_back_kernel(
    scal, q_ref, r0, r1, r2, r3, lo_ref, att_ref, log_ref, d_ref, cos_ref, sin_ref, dq_ref, bias_ref, keep_near, keep_far, give_near, give_far, acc, delta
):
    refs = (r0, r1, r2, r3)
    rows, width = q_ref.shape
    hd = r0.shape[2]
    heads = width // hd
    scale = hd**-0.5
    factor = LOG2E * scale
    acc[...] = jnp.zeros_like(acc)
    for h in range(heads):
        cols = slice(h * hd, (h + 1) * hd)
        both = d_ref[:, cols].astype(F32) * att_ref[:, cols].astype(F32)
        delta[h] = jnp.broadcast_to(jnp.sum(both.T, axis=0, keepdims=True), delta.shape[1:])
    zero = jnp.zeros((rows, hd), BF16)

    def put(b, keep, give):
        nz = keep_near.shape[0]
        z = lax.rem(lax.div(b, 2) - lax.div(scal[0], 2) + nz, nz)
        near = lax.rem(b, 2) == lax.rem(scal[0], 2)

        @pl.when(near)
        def _():
            keep_near[z] = keep
            give_near[z] = give

        @pl.when(jnp.logical_not(near))
        def _():
            keep_far[z] = keep
            give_far[z] = give

    def clear(b, carry):
        put(b, zero, zero)
        return carry

    start, stop = block_bounds(scal, rows)
    lax.fori_loop(0, start, clear, 0)
    lax.fori_loop(stop, 2 * keep_near.shape[0], clear, 0)

    def run(b, masked):
        kb, vb = key_value(scal, refs, b, rows)
        kt = kb.astype(F32).T.astype(BF16)
        dk = jnp.zeros((rows, hd), F32)
        dv = jnp.zeros((rows, hd), F32)
        for h in range(heads):
            cols = slice(h * hd, (h + 1) * hd)
            qh = q_ref[:, cols]
            dh = d_ref[:, cols]
            p = probs_t(scal, kb, qh, lo_ref[...], b, rows, factor, log_ref[h, 0:1, :], masked)
            dp = mm(vb, dh, 1, 1)
            ds = (p * (dp - delta[h, 0:1, :])).astype(BF16)
            dv += mm(p.astype(BF16), dh, 1, 0)
            dk += mm(ds, qh, 1, 0)
            acc[h] += mm(kt, ds, 1, 0)
        dk = (dk * scale).astype(BF16)
        dv = dv.astype(BF16)
        put(b, jnp.where(scal[3] == 0, dk, dv), jnp.where(scal[3] == 0, dv, dk))

    for_blocks(scal, rows, run)
    for h in range(heads):
        dq = (acc[h] * scale).T
        dq = dq * cos_ref[...] + pltpu.roll(dq, hd // 2, 1) * sin_ref[...]
        dq = dq.astype(BF16)
        dq_ref[:, h * hd : (h + 1) * hd] = dq
        bias_ref[:, h * hd : (h + 1) * hd] = jnp.sum(dq.astype(F32), axis=0, keepdims=True)


VMEM = pl.BlockSpec(memory_space=pltpu.VMEM)
SMEM = pl.BlockSpec(memory_space=pltpu.SMEM)
ANYWHERE = pl.BlockSpec(memory_space=pl.ANY)
MIB = 1024 * 1024


def cost(us):
    return pl.CostEstimate(flops=int(us * 1.15e9), bytes_accessed=0, transcendentals=0)


def attend(scal, q, kv, lo):
    rows, width = q.shape
    hd = kv[0].shape[2]
    heads = width // hd
    return pl.pallas_call(
        attend_kernel,
        in_specs=[SMEM] + [VMEM] * 6,
        out_specs=[VMEM, VMEM],
        out_shape=[
            jax.ShapeDtypeStruct((rows, width), BF16),
            jax.ShapeDtypeStruct((heads, 8, rows), F32),
        ],
        scratch_shapes=[pltpu.VMEM((heads, hd, rows), F32), pltpu.VMEM((heads, 8, rows), F32)],
        compiler_params=pltpu.CompilerParams(vmem_limit_bytes=20 * MIB),
        cost_estimate=cost(50),
        name="attend",
    )(scal, q, *kv, lo)


def attend_back(scal, q, kv, lo, att, logs, d_att, cos, sin):
    rows, width = q.shape
    hd = kv[0].shape[2]
    heads = width // hd
    grads = jax.ShapeDtypeStruct(kv[0].shape[:1] + (rows, hd), BF16)
    return pl.pallas_call(
        attend_back_kernel,
        in_specs=[SMEM] + [VMEM] * 11,
        out_specs=[VMEM] * 6,
        out_shape=[
            jax.ShapeDtypeStruct((rows, width), BF16),
            jax.ShapeDtypeStruct((1, width), F32),
            *([grads] * 4),
        ],
        scratch_shapes=[pltpu.VMEM((heads, hd, rows), F32), pltpu.VMEM((heads, 8, rows), F32)],
        compiler_params=pltpu.CompilerParams(vmem_limit_bytes=26 * MIB),
        cost_estimate=cost(8),
        name="attend_back",
    )(scal, q, *kv, lo, att, logs, d_att, cos, sin)


CHUNK = 512


def column_fetch(scal, quarters, nz, quarter, rows, normed, nbuf, nsem, cots=None, cbuf=None, csem=None):
    z, core, y = scal[1], lax.rem(scal[2], 2), lax.div(scal[2], 2)
    per_chunk = CHUNK // quarter
    chunks = [(k, first) for k in range(quarters) for first in range(0, nz, per_chunk)]

    def fetch(c):
        k, first = chunks[c]
        slot = c % nbuf.shape[0]
        q = 2 * ((1 - y) if k % 2 else y) + ((1 - core) if k // 2 else core)
        for i in range(per_chunk):
            dist = first + i
            row = pl.multiple_of(lax.rem(z - dist + nz, nz) * rows + q * quarter, quarter)
            place = pl.ds(i * quarter, quarter)
            pltpu.make_async_copy(normed.at[pl.ds(row, quarter), :], nbuf.at[slot, place, :], nsem.at[slot]).start()
            if cots is None:
                continue
            if dist == 0:
                source = cots[0].at[pl.ds(pl.multiple_of(q * quarter, quarter), quarter), :]
            else:
                source = cots[k + 1].at[pl.ds((dist - 1) * quarter, quarter), :]
            pltpu.make_async_copy(source, cbuf.at[slot, place, :], csem.at[slot]).start()

    for c in range(min(nbuf.shape[0], len(chunks))):
        fetch(c)
    return fetch, len(chunks)


def column_put(scal, acc, keep, give):
    nz, part, _ = keep.shape
    flat = acc[...].T.astype(BF16)
    for i in range(2 * nz):
        value = flat[i * part : (i + 1) * part, :]
        dist = lax.rem(i // 2 - scal[1] + nz, nz)

        @pl.when(scal[0] == i % 2)
        def _(value=value, dist=dist):
            keep[dist] = value

        @pl.when(scal[0] != i % 2)
        def _(value=value, dist=dist):
            give[dist] = value


def column_first_kernel(quarters, scal, normed, *refs):
    cots = refs[: quarters + 1]
    gate_ref, up_ref, down_ref, kd, gd, d_gate_ref, d_up_ref = refs[quarters + 1 : quarters + 8]
    nbuf, cbuf, ad, nsem, csem = refs[quarters + 8 :]
    rows = cots[0].shape[0]
    fetch, count = column_fetch(
        scal, quarters, kd.shape[0], rows // quarters, rows, normed, nbuf, nsem, cots, cbuf, csem
    )
    slots = nbuf.shape[0]
    for c in range(count):
        slot = c % slots
        place = slice(c * CHUNK, (c + 1) * CHUNK)
        pltpu.make_async_copy(nbuf.at[slot], nbuf.at[slot], nsem.at[slot]).wait()
        pltpu.make_async_copy(cbuf.at[slot], cbuf.at[slot], csem.at[slot]).wait()
        gate = mm(gate_ref[...], nbuf[slot], 1, 1)
        up = mm(up_ref[...], nbuf[slot], 1, 1)
        d_hidden = mm(down_ref[...], cbuf[slot], 1, 1)
        sig = 1.0 / (1.0 + jnp.exp(-gate))
        silu = gate * sig
        hidden = (silu * up).astype(BF16)
        d_gate_ref[:, place] = (d_hidden * up * sig * (1.0 + gate * (1.0 - sig))).astype(BF16)
        d_up_ref[:, place] = (d_hidden * silu).astype(BF16)
        grad = mm(hidden, cbuf[slot], 1, 0)
        ad[...] = grad if c == 0 else ad[...] + grad
        if c + slots < count:
            fetch(c + slots)
    column_put(scal, ad, kd, gd)


def column_second_kernel(quarters, rows, scal, normed, d_gate_ref, d_up_ref, kg, gg, ku, gu, nbuf, ag, au, nsem):
    fetch, count = column_fetch(scal, quarters, kg.shape[0], rows // quarters, rows, normed, nbuf, nsem)
    slots = nbuf.shape[0]
    for c in range(count):
        slot = c % slots
        place = slice(c * CHUNK, (c + 1) * CHUNK)
        pltpu.make_async_copy(nbuf.at[slot], nbuf.at[slot], nsem.at[slot]).wait()
        for acc, left in ((ag, d_gate_ref), (au, d_up_ref)):
            grad = mm(left[:, place], nbuf[slot], 1, 0)
            acc[...] = grad if c == 0 else acc[...] + grad
        if c + slots < count:
            fetch(c + slots)
    column_put(scal, ag, kg, gg)
    column_put(scal, au, ku, gu)


def column_first(scal, normed, cots, gate_s, up_s, down_s, n):
    unit, width = gate_s.shape
    quarters = len(cots) - 1
    tokens = normed.shape[0]
    slots = min(tokens // CHUNK, 4)
    out = jax.ShapeDtypeStruct((n // 2, width // n, unit), BF16)
    units = jax.ShapeDtypeStruct((unit, tokens), BF16)
    return pl.pallas_call(
        functools.partial(column_first_kernel, quarters),
        in_specs=[SMEM] + [ANYWHERE] * (quarters + 2) + [VMEM] * 3,
        out_specs=[VMEM] * 4,
        out_shape=[out] * 2 + [units] * 2,
        scratch_shapes=[pltpu.VMEM((slots, CHUNK, width), BF16)] * 2
        + [pltpu.VMEM((unit, width), F32)]
        + [pltpu.SemaphoreType.DMA((slots,))] * 2,
        compiler_params=pltpu.CompilerParams(vmem_limit_bytes=50 * MIB),
        cost_estimate=cost(14),
        name="column_first",
    )(scal, normed, *cots, gate_s, up_s, down_s)


def column_second(scal, normed, d_gate, d_up, rows, n):
    unit, tokens = d_gate.shape
    width = normed.shape[1]
    slots = min(tokens // CHUNK, 4)
    out = jax.ShapeDtypeStruct((n // 2, width // n, unit), BF16)
    return pl.pallas_call(
        functools.partial(column_second_kernel, 4, rows),
        in_specs=[SMEM, ANYWHERE, VMEM, VMEM],
        out_specs=[VMEM] * 4,
        out_shape=[out] * 4,
        scratch_shapes=[pltpu.VMEM((slots, CHUNK, width), BF16)]
        + [pltpu.VMEM((unit, width), F32)] * 2
        + [pltpu.SemaphoreType.DMA((slots,))],
        compiler_params=pltpu.CompilerParams(vmem_limit_bytes=40 * MIB),
        cost_estimate=cost(10),
        name="column_second",
    )(scal, normed, d_gate, d_up)


FF_STEPS = 4


def mlp_kernel(scal, n_ref, dh_ref, gate_ref, up_ref, hidden_ref, d_keep, d_give, d_acc):
    step = pl.program_id(0)
    gate = mm(gate_ref[...], n_ref[...], 1, 1)
    up = mm(up_ref[...], n_ref[...], 1, 1)
    d_hidden = dh_ref[...].astype(F32)
    sig = 1.0 / (1.0 + jnp.exp(-gate))
    silu = gate * sig
    hidden_ref[...] = (silu * up).astype(BF16)
    d_gate = (d_hidden * up * sig * (1.0 + gate * (1.0 - sig))).astype(BF16)
    d_up = (d_hidden * silu).astype(BF16)
    d_normed = mm(d_gate, gate_ref[...], 0, 0) + mm(d_up, up_ref[...], 0, 0)

    @pl.when(step == 0)
    def _():
        d_acc[...] = d_normed

    @pl.when(step > 0)
    def _():
        d_acc[...] += d_normed

    @pl.when(step == FF_STEPS - 1)
    def _():
        halves(scal[0], d_acc, d_keep, d_give)


def mlp(core, normed, d_hidden, gate_t, up_t):
    rows, width = normed.shape
    ff = gate_t.shape[0]
    units = pl.BlockSpec((ff // FF_STEPS, width), lambda i: (i, 0))
    tokens = pl.BlockSpec((ff // FF_STEPS, rows), lambda i: (i, 0))
    return pl.pallas_call(
        mlp_kernel,
        grid=(FF_STEPS,),
        in_specs=[SMEM, VMEM, tokens, units, units],
        out_specs=[tokens, VMEM, VMEM],
        out_shape=[
            jax.ShapeDtypeStruct((ff, rows), BF16),
            jax.ShapeDtypeStruct((rows // 2, width), F32),
            jax.ShapeDtypeStruct((rows // 2, width), BF16),
        ],
        scratch_shapes=[pltpu.VMEM((rows, width), F32)],
        compiler_params=pltpu.CompilerParams(vmem_limit_bytes=40 * MIB, dimension_semantics=("arbitrary",)),
        cost_estimate=cost(12),
        name="mlp",
    )(core.reshape(1).astype(jnp.int32), normed, d_hidden, gate_t, up_t)


def halves(core, total, keep, give):
    half = total.shape[0] // 2
    keep[...] = total[pl.ds(pl.multiple_of(core * half, half), half), :]
    give[...] = total[pl.ds(pl.multiple_of((1 - core) * half, half), half), :].astype(BF16)


def project_kernel(scal, *refs):
    count = len(refs) - 11
    ring, (cos_ref, sin_ref, q_ref, qw_ref, kvw_ref, n_ref) = refs[:count], refs[count : count + 6]
    kv_ref, sum_ref, keep, give, total = refs[count + 6 :]
    rows = q_ref.shape[0]
    d_kv = ring[0][0:rows, :].astype(F32)
    for piece in ring[1:]:
        d_kv += piece[0:rows, :].astype(F32)
    turned = d_kv * cos_ref[...] + pltpu.roll(d_kv, d_kv.shape[1] // 2, 1) * sin_ref[...]
    d_kv = jnp.where(scal[0] == 0, turned, d_kv).astype(BF16)
    kv_ref[...] = mm(n_ref[...], d_kv, 0, 0).astype(BF16)
    sum_ref[...] = jnp.sum(d_kv.astype(F32), axis=0, keepdims=True)
    total[...] = mm(q_ref[...], qw_ref[...], 1, 1) + mm(d_kv, kvw_ref[...], 1, 1)
    halves(scal[0], total, keep, give)


def output_kernel(scal, h_ref, down_ref, keep, give, total):
    total[...] = mm(h_ref[...], down_ref[...], 0, 0)
    halves(scal[0], total, keep, give)


def halves_shapes(rows, width):
    return [jax.ShapeDtypeStruct((rows // 2, width), F32), jax.ShapeDtypeStruct((rows // 2, width), BF16)]


def project(core, ring, cos, sin, d_query, q_weight, kv_cols, normed):
    rows, width = d_query.shape[0], q_weight.shape[0]
    return pl.pallas_call(
        project_kernel,
        in_specs=[SMEM] + [VMEM] * (len(ring) + 6),
        out_specs=[VMEM] * 4,
        out_shape=[
            jax.ShapeDtypeStruct((width, ring[0].shape[1]), BF16),
            jax.ShapeDtypeStruct((1, ring[0].shape[1]), F32),
            *halves_shapes(rows, width),
        ],
        scratch_shapes=[pltpu.VMEM((rows, width), F32)],
        compiler_params=pltpu.CompilerParams(vmem_limit_bytes=24 * MIB),
        cost_estimate=cost(30),
        name="project",
    )(core.reshape(1).astype(jnp.int32), *ring, cos, sin, d_query, q_weight, kv_cols, normed)


def project_output(core, hidden, down):
    rows, width = hidden.shape[1], down.shape[1]
    return pl.pallas_call(
        output_kernel,
        in_specs=[SMEM] + [VMEM] * 2,
        out_specs=[VMEM] * 2,
        out_shape=halves_shapes(rows, width),
        scratch_shapes=[pltpu.VMEM((rows, width), F32)],
        compiler_params=pltpu.CompilerParams(vmem_limit_bytes=30 * MIB),
        cost_estimate=cost(30),
        name="project_output",
    )(core.reshape(1).astype(jnp.int32), hidden, down)


def norm_back_kernel(x_ref, gain_ref, dn_ref, base_ref, dx_ref, gain_grad_ref):
    values = x_ref[...].astype(F32)
    factor = lax.rsqrt(jnp.mean(values * values, axis=-1, keepdims=True) + RMS_EPS)
    w = values * factor
    dn = dn_ref[...].astype(F32)
    gain_grad_ref[...] = jnp.sum(dn * w, axis=0, keepdims=True)
    dg = dn * gain_ref[...].astype(F32)
    dx_ref[...] = base_ref[...] + factor * (dg - w * jnp.mean(dg * w, axis=-1, keepdims=True))


def norm_back(x, gain, dn, base):
    rows, width = x.shape
    return pl.pallas_call(
        norm_back_kernel,
        in_specs=[VMEM] * 4,
        out_specs=[VMEM] * 2,
        out_shape=[jax.ShapeDtypeStruct((rows, width), F32), jax.ShapeDtypeStruct((1, width), F32)],
        compiler_params=pltpu.CompilerParams(vmem_limit_bytes=24 * MIB),
        cost_estimate=cost(30),
        name="norm_back",
    )(x, gain.reshape(1, width), dn, base)


def assemble_kernel(nz, scal, *refs):
    unit = refs[0].shape[1]
    groups, targets = (refs[:nz], refs[nz : 2 * nz], refs[2 * nz : 3 * nz]), refs[3 * nz :]

    def block(group, j):
        dist = lax.rem(scal[1] - j + nz, nz)
        value = group[0][...]
        for d in range(1, nz):
            value = jnp.where(dist == d, group[d][...], value)
        return value.astype(F32)

    for group, target in zip(groups, targets):
        target[...] = jnp.concatenate([block(group, j) for j in range(nz)], axis=1)


def assemble(scal, gate, up, down):
    nz = len(gate)
    part, unit = gate[0].shape
    ff = nz * unit
    return pl.pallas_call(
        functools.partial(assemble_kernel, nz),
        in_specs=[SMEM] + [VMEM] * (3 * nz),
        out_specs=[VMEM] * 3,
        out_shape=[jax.ShapeDtypeStruct((part, ff), F32)] * 3,
        compiler_params=pltpu.CompilerParams(vmem_limit_bytes=28 * MIB),
        cost_estimate=cost(5),
        name="assemble",
    )(scal, *gate, *up, *down)


def per_device(
    layer_input,
    segment_ids,
    positions,
    attn_gain,
    q_weight,
    q_bias,
    kv_weight,
    kv_bias,
    o_weight,
    mlp_gain,
    gate_weight,
    up_weight,
    down_weight,
    cotangent,
):
    rows, width = layer_input.shape
    heads, hd = q_bias.shape
    ff = gate_weight.shape[1]
    nz, x, y, core = lax.axis_size("z"), lax.axis_index("x"), lax.axis_index("y"), lax.axis_index("core")
    z = lax.axis_index("z")
    n, ntp = 2 * nz, 4
    ctx = 2 * z + x
    tp = 2 * y + core
    unit = ff // nz

    o_full = jnp.concatenate(gather_tp(o_weight, core, y), axis=0)
    gate_s = lax.dynamic_slice_in_dim(gate_weight.T, z * unit, unit, 0)
    up_s = lax.dynamic_slice_in_dim(up_weight.T, z * unit, unit, 0)
    down_s = lax.dynamic_slice_in_dim(down_weight, z * unit, unit, 0)

    inputs = layer_input.astype(F32)
    gain_one = attn_gain.astype(F32)
    factor_one = lax.rsqrt(jnp.mean(inputs * inputs, axis=-1, keepdims=True) + RMS_EPS)
    normed = (inputs * factor_one * gain_one).astype(BF16)
    cosine, sine = rope_tables(positions, hd)
    cos_back = jnp.concatenate([cosine, cosine], axis=1)
    sin_back = jnp.concatenate([sine, -sine], axis=1)
    query = mm(normed, q_weight, 1, 0) + q_bias.astype(F32).reshape(-1)
    query_rot = rotate(query.reshape(rows, heads, hd), cosine[:, None], sine[:, None])
    query_rot = query_rot.astype(BF16).reshape(rows, heads * hd)
    column = (2 * core + y) * hd
    kv_cols = lax.dynamic_slice_in_dim(kv_weight, column, hd, 1)
    kv_own_bias = lax.dynamic_slice_in_dim(kv_bias, column, hd, 0).astype(F32)
    kv_own = mm(normed, kv_cols, 1, 0) + kv_own_bias
    kv_own = jnp.where(core == 0, rotate(kv_own, cosine, sine), kv_own).astype(BF16)

    ids = segment_ids.astype(BF16).reshape(rows // hd, hd)
    ids = jnp.pad(ids, ((0, EXTRA - rows // hd), (0, 0)))
    packed = jnp.concatenate([kv_own, ids], axis=0)
    near = lax.all_to_all(
        jnp.broadcast_to(packed[None], (nz,) + packed.shape), "z", split_axis=0, concat_axis=0, tiled=True
    )
    quarter = rows // ntp
    cot_own = lax.dynamic_slice_in_dim(after(cotangent, near), tp * quarter, quarter, 0)
    cot_ahead = [along_z(cot_own, 1)]
    far = swap(near, "x")
    kv = (near, far, swap(near, "core"), swap(far, "core"))
    kv, gate_s, up_s, down_s = lax.optimization_barrier((kv, gate_s, up_s, down_s))
    all_ids = jnp.stack([near[:, rows : rows + rows // hd], far[:, rows : rows + rows // hd]]).astype(F32)
    starts = [jnp.sum((all_ids < k).astype(F32)).astype(jnp.int32) for k in (1, 2, 3)]
    lo = jnp.where(
        segment_ids == 0,
        0,
        jnp.where(segment_ids == 1, starts[0], jnp.where(segment_ids == 2, starts[1], starts[2])),
    )
    scal = jnp.stack([ctx, lo[0], lo[-1], core]).astype(jnp.int32)
    lo = lo.reshape(1, rows)

    attended, logs = attend(scal, query_rot, kv, lo)
    attended, logs, cot_ahead = lax.optimization_barrier((attended, logs, cot_ahead))
    cot_ahead += [along_z(cot_ahead[-1], 1)]
    d_hidden = mm(down_weight, after(cotangent, attended), 1, 1).astype(BF16)
    attended_all = jnp.concatenate(gather_tp(attended, core, y), axis=1)
    attended_all, d_hidden, cot_ahead = lax.optimization_barrier((attended_all, d_hidden, cot_ahead))
    while len(cot_ahead) < nz - 1:
        cot_ahead += [along_z(cot_ahead[-1], 1)]
    hidden_in = inputs + mm(attended_all, o_full, 1, 0)

    gain_two = mlp_gain.astype(F32)
    factor_two = lax.rsqrt(jnp.mean(hidden_in * hidden_in, axis=-1, keepdims=True) + RMS_EPS)
    normed_two = (hidden_in * factor_two * gain_two).astype(BF16)
    normed_all = column_tokens(normed_two, core)

    hidden, d_keep, d_give = mlp(core, normed_two, d_hidden, gate_weight.T, up_weight.T)
    hidden, d_keep, d_give, cot_ahead = lax.optimization_barrier((hidden, d_keep, d_give, cot_ahead))
    d_half = sum_y(sum_core(d_keep, d_give))
    cot_here = jnp.concatenate(after(cot_ahead, d_half), axis=0)
    cot_there = swap(cot_here, "y")
    d_normed_two = join_core(d_half, core).astype(F32)

    w_two = hidden_in * factor_two
    part_mlp_gain = jnp.sum(d_normed_two * w_two, axis=0)
    dg_two = d_normed_two * gain_two
    d_hidden_in = cotangent.astype(F32) + factor_two * (
        dg_two - w_two * jnp.mean(dg_two * w_two, axis=-1, keepdims=True)
    )
    d_attn = d_hidden_in.astype(BF16)
    d_attended = mm(d_attn, o_weight, 1, 1).astype(BF16)
    part, small = width // n, width // (n * ntp)
    g_o = mm(d_attn, attended, 0, 0).astype(BF16).reshape(nz, 2, part, heads * hd).swapaxes(0, 1)
    keep_o = lax.dynamic_index_in_dim(g_o, x, 0, keepdims=False)
    give_o = lax.dynamic_index_in_dim(g_o, 1 - x, 0, keepdims=False)
    d_attended, keep_o, give_o = lax.optimization_barrier((d_attended, keep_o, give_o))
    came_o = swap(give_o, "x")

    back = attend_back(scal, query_rot, kv, lo, attended, logs, d_attended, cos_back, sin_back)
    back, came_o, cot_there = lax.optimization_barrier((back, came_o, cot_there))
    d_query, q_bias_sum, keep_near, keep_far, give_near, give_far = back
    cots = (cotangent, cot_here, cot_there, swap(cot_here, "core"), swap(cot_there, "core"))
    d_far = (keep_far.astype(F32) + swap(give_far, "core").astype(F32)).astype(BF16)
    came_near = swap(give_near, "core")
    g_q = mm(normed, after(d_query, d_far), 0, 0).astype(BF16).reshape(nz, 2, part, heads * hd)
    keep_q = lax.dynamic_index_in_dim(g_q, x, 1, keepdims=False)
    give_q = lax.dynamic_index_in_dim(g_q, 1 - x, 1, keepdims=False)
    g_o = by_distance((keep_o.astype(F32) + came_o.astype(F32)).astype(BF16), z)
    came_near, d_far, keep_q, give_q, g_o, normed_all, cots = lax.optimization_barrier(
        (came_near, d_far, keep_q, give_q, g_o, normed_all, cots)
    )
    came_far, came_q, g_o = swap(d_far, "x"), swap(give_q, "x"), spread(g_o)

    place = jnp.stack([x, z, tp]).astype(jnp.int32)
    keep_down, give_down, d_gate_c, d_up_c = column_first(place, normed_all, cots, gate_s, up_s, down_s, n)
    came_far, came_q, g_o, d_gate_c, give_down = lax.optimization_barrier((came_far, came_q, g_o, d_gate_c, give_down))
    ring = [
        (keep_near[s].astype(F32) + came_near[s].astype(F32) + came_far[s].astype(F32)).astype(BF16)
        for s in range(nz)
    ]
    g_q = by_distance((keep_q.astype(F32) + came_q.astype(F32)).astype(BF16), z)
    ring = [
        jnp.concatenate([ring[s]] + [g_q[s][:, h * hd : (h + 1) * hd] for h in range(heads)], axis=0)
        for s in range(nz)
    ]
    ring, d_gate_c = lax.optimization_barrier((ring, d_gate_c))
    ring = spread(ring)
    came_down = swap(give_down, "x")
    keep_gate, give_gate, keep_up, give_up = column_second(place, normed_all, d_gate_c, d_up_c, rows, n)
    came_down, ring, give_gate, give_up = lax.optimization_barrier((came_down, ring, give_gate, give_up))

    sums, give_gate, ring = lax.optimization_barrier((sum_parts(keep_down, came_down), give_gate, ring))
    came_gate, g_down = swap(give_gate, "x"), spread(sums)
    parts = project(core, ring, cos_back, sin_back, d_query, q_weight, kv_cols, normed)
    parts, came_gate, g_down = lax.optimization_barrier((parts, came_gate, g_down))
    g_kv, d_kv_sum = parts[0].reshape(n * ntp, small, hd), parts[1]
    sums, give_up, parts = lax.optimization_barrier((sum_parts(keep_gate, came_gate), give_up, parts))
    came_up, g_gate = swap(give_up, "x"), spread(sums)
    d_half = sum_core(*parts[2:])
    hidden, d_half = lax.optimization_barrier((hidden, d_half))
    came_half = swap(d_half, "y")
    o_parts = project_output(core, hidden, down_weight)
    o_parts, came_up, g_gate, came_half = lax.optimization_barrier((o_parts, came_up, g_gate, came_half))
    d_normed = (d_half.astype(F32) + came_half.astype(F32)).astype(BF16)
    sums, d_normed, o_parts = lax.optimization_barrier((sum_parts(keep_up, came_up), d_normed, o_parts))
    g_up = spread(sums)
    o_half = sum_core(*o_parts)
    d_normed = join_core(d_normed, core)
    d_normed, o_half = lax.optimization_barrier((d_normed, o_half))
    came_o_half = swap(o_half, "y")
    dx, part_attn_gain = norm_back(layer_input, attn_gain, d_normed, d_hidden_in)
    dx, part_attn_gain, g_up, came_o_half = lax.optimization_barrier((dx, part_attn_gain, g_up, came_o_half))
    o_half = (o_half.astype(F32) + came_o_half.astype(F32)).astype(BF16)
    output = (hidden_in + join_core(o_half, core).astype(F32)).astype(BF16)

    bias_cols = hd // n
    tail_rows = jnp.concatenate(
        [
            jnp.broadcast_to(d_kv_sum, (n, hd)),
            part_mlp_gain.reshape(n, part),
            part_attn_gain.reshape(n, part),
            jnp.broadcast_to(q_bias_sum, (n, heads * hd)),
        ],
        axis=1,
    )
    extra = -(-tail_rows.shape[1] // (EXTRA * hd)) * EXTRA
    tail_rows = jnp.pad(tail_rows, ((0, 0), (0, extra * hd - tail_rows.shape[1]))).astype(BF16)
    tail_rows = jnp.broadcast_to(tail_rows.reshape(n, 1, extra, hd), (n, ntp, extra, hd)).reshape(-1, extra, hd)
    g_kv = lax.all_to_all(
        jnp.concatenate([g_kv, tail_rows], axis=1), ("z", "x", "y", "core"), split_axis=0, concat_axis=0, tiled=True
    )
    g_kv = jnp.sum(g_kv.reshape(n, ntp, small + extra, hd).astype(F32), axis=0)
    sums = lax.dynamic_index_in_dim(g_kv[:, small:], tp, 0, keepdims=False).reshape(-1)[hd:]
    g_mlp_gain = sums[:part]
    g_attn_gain = sums[part : 2 * part]
    g_q_bias = sums[2 * part : 2 * part + heads * hd].reshape(heads, hd)
    g_q_bias = lax.dynamic_slice_in_dim(g_q_bias, ctx * bias_cols, bias_cols, 1)
    g_kv = jnp.concatenate([g_kv[0], g_kv[2], g_kv[1], g_kv[3]], axis=1)
    bias_size = kv_bias.shape[0] // (n * ntp)
    g_kv_bias = lax.dynamic_slice_in_dim(g_kv[small], (ctx * ntp + tp) * bias_size, bias_size, 0)
    g_kv = g_kv[:small]

    g_gate, g_up, g_down = assemble(place, g_gate, g_up, g_down)
    g_down = g_down.T
    g_o = sum(g.astype(F32) for g in after(g_o, g_up)).T
    g_q = sum(r[rows:].astype(F32) for r in ring).reshape(heads, part, hd).transpose(1, 0, 2).reshape(part, heads * hd)

    return (
        output,
        dx,
        g_attn_gain,
        g_q,
        g_q_bias,
        g_kv,
        g_kv_bias,
        g_o,
        g_mlp_gain,
        g_gate,
        g_up,
        g_down,
    )


def solution(mesh):
    n, ntp = mesh.shape["ctx"], mesh.shape["tp"]
    fine = jax.sharding.Mesh(mesh.devices.reshape(n // 2, 2, ntp // 2, 2), ("z", "x", "y", "core"))
    ctx, tp = ("z", "x"), ("y", "core")
    both = ctx + tp
    return jax.shard_map(
        per_device,
        mesh=fine,
        in_specs=(
            P(ctx, None),
            P(ctx),
            P(ctx),
            P(),
            P(None, tp),
            P(tp, None),
            P(),
            P(),
            P(tp, None),
            P(),
            P(None, tp),
            P(None, tp),
            P(tp, None),
            P(ctx, None),
        ),
        out_specs=(
            P(ctx, None),
            P(ctx, None),
            P(ctx),
            P(ctx, tp),
            P(tp, ctx),
            P(both, None),
            P(both),
            P(tp, ctx),
            P(ctx),
            P(ctx, tp),
            P(ctx, tp),
            P(tp, ctx),
        ),
        check_vma=False,
    )
```

```python
import functools

import jax
import jax.numpy as jnp
from jax import lax
from jax.experimental import pallas as pl
from jax.experimental.pallas import tpu as pltpu
from jax.sharding import PartitionSpec as P

RMS_EPS = 1e-06
ROPE_BASE = 1000000.0
LOG2E = 1.4426950408889634
BF16 = jnp.bfloat16
F32 = jnp.float32
EXTRA = 16


def mm(a, b, ca, cb):
    return lax.dot_general(a, b, (((ca,), (cb,)), ((), ())), preferred_element_type=F32)


def rope_tables(positions, head_dim):
    half = head_dim // 2
    freqs = ROPE_BASE ** (-2.0 * jnp.arange(half, dtype=F32) / head_dim)
    angles = positions.astype(F32)[:, None] * freqs[None, :]
    return jnp.cos(angles), jnp.sin(angles)


def rotate(values, cosine, sine):
    half = cosine.shape[-1]
    first, second = values[..., :half], values[..., half:]
    return jnp.concatenate([first * cosine - second * sine, second * cosine + first * sine], axis=-1)


def swap(x, axis):
    return lax.ppermute(x, axis, [(0, 1), (1, 0)])


def gather_tp(x, core, y):
    far = swap(x, "y")
    mate = swap(x, "core")
    far_mate = swap(far, "core")
    a0, a1 = jnp.where(core == 0, x, mate), jnp.where(core == 0, mate, x)
    b0, b1 = jnp.where(core == 0, far, far_mate), jnp.where(core == 0, far_mate, far)
    return [
        jnp.where(y == 0, a0, b0),
        jnp.where(y == 0, a1, b1),
        jnp.where(y == 0, b0, a0),
        jnp.where(y == 0, b1, a1),
    ]


def sum_core(keep, give):
    return (keep + swap(give, "core").astype(F32)).astype(BF16)


def sum_y(half):
    return (half.astype(F32) + swap(half, "y").astype(F32)).astype(BF16)


def join_core(half, core):
    mate = swap(half, "core")
    return jnp.concatenate([jnp.where(core == 0, half, mate), jnp.where(core == 0, mate, half)], axis=0)


def split_core(part, core):
    rows = part.shape[0] // 2
    keep = lax.dynamic_slice_in_dim(part, core * rows, rows, 0)
    return keep, lax.dynamic_slice_in_dim(part, (1 - core) * rows, rows, 0).astype(BF16)


def sum_x(parts, x):
    keep = lax.dynamic_index_in_dim(parts, x, 0, keepdims=False)
    give = lax.dynamic_index_in_dim(parts, 1 - x, 0, keepdims=False)
    return (keep.astype(F32) + swap(give, "x").astype(F32)).astype(BF16)


def by_distance(parts, z):
    nz = parts.shape[0]
    return [lax.dynamic_index_in_dim(parts, lax.rem(z + s, nz), 0, keepdims=False) for s in range(nz)]


def sum_parts(keep, came):
    return [(keep[s].astype(F32) + came[s].astype(F32)).astype(BF16) for s in range(keep.shape[0])]


def spread(sums):
    return sums[:1] + [along_z(sums[s], s) for s in range(1, len(sums))]


def along_z(block, distance):
    nz = lax.axis_size("z")
    return lax.ppermute(block, "z", [(i, (i + distance) % nz) for i in range(nz)])


def column_tokens(block, core):
    half = block.shape[0] // 2
    own = lax.dynamic_slice_in_dim(block, core * half, half, 0)
    return lax.all_gather(own, ("z", "core"), axis=0, tiled=True)


def after(values, *done):
    return lax.optimization_barrier((values, done))[0]


def block_bounds(scal, rows):
    return lax.div(scal[1], rows), scal[0] + 1


def probs_t(scal, kb, qh, lo_row, b, rows, factor, shift, masked):
    s = mm(kb, qh, 1, 1) * factor
    if shift is not None:
        s = s - shift
    p = jnp.exp2(s)
    if masked:
        key = b * rows + lax.broadcasted_iota(jnp.int32, p.shape, 0)
        query = scal[0] * p.shape[1] + lax.broadcasted_iota(jnp.int32, p.shape, 1)
        p = jnp.where((key <= query) & (key >= lo_row), p, 0.0)
    return p


def for_blocks(scal, rows, run):
    start, stop = block_bounds(scal, rows)

    def body(b, carry):
        plain = (b < scal[0]) & (scal[2] <= b * rows)

        @pl.when(plain)
        def _():
            run(b, False)

        @pl.when(jnp.logical_not(plain))
        def _():
            run(b, True)

        return carry

    lax.fori_loop(start, stop, body, 0)


def key_value(scal, refs, b, rows):
    z = lax.div(b, 2)
    near = lax.rem(b, 2) == lax.rem(scal[0], 2)
    mine = jnp.where(near, refs[0][z, 0:rows, :], refs[1][z, 0:rows, :])
    other = jnp.where(near, refs[2][z, 0:rows, :], refs[3][z, 0:rows, :])
    return jnp.where(scal[3] == 0, mine, other), jnp.where(scal[3] == 0, other, mine)


def attend_kernel(scal, q_ref, r0, r1, r2, r3, lo_ref, att_ref, log_ref, acc, tot):
    refs = (r0, r1, r2, r3)
    rows, width = q_ref.shape
    hd = r0.shape[2]
    heads = width // hd
    factor = LOG2E * hd**-0.5
    acc[...] = jnp.zeros_like(acc)
    tot[...] = jnp.zeros_like(tot)

    def run(b, masked):
        kb, vb = key_value(scal, refs, b, rows)
        vt = vb.astype(F32).T.astype(BF16)
        for h in range(heads):
            p = probs_t(
                scal, kb, q_ref[:, h * hd : (h + 1) * hd], lo_ref[...], b, rows, factor, None, masked
            )
            tot[h] += jnp.sum(p.reshape(rows // 8, 8, p.shape[1]), axis=0)
            acc[h] += mm(vt, p.astype(BF16), 1, 0)

    for_blocks(scal, rows, run)
    for h in range(heads):
        total = jnp.sum(tot[h], axis=0, keepdims=True)
        att_ref[:, h * hd : (h + 1) * hd] = (acc[h] / total).T.astype(BF16)
        log_ref[h] = jnp.broadcast_to(jnp.log2(total), log_ref.shape[1:])


def attend_back_kernel(
    scal, q_ref, r0, r1, r2, r3, lo_ref, att_ref, log_ref, d_ref, cos_ref, sin_ref, dq_ref, bias_ref, keep_near, keep_far, give_near, give_far, acc, delta
):
    refs = (r0, r1, r2, r3)
    rows, width = q_ref.shape
    hd = r0.shape[2]
    heads = width // hd
    scale = hd**-0.5
    factor = LOG2E * scale
    acc[...] = jnp.zeros_like(acc)
    for h in range(heads):
        cols = slice(h * hd, (h + 1) * hd)
        both = d_ref[:, cols].astype(F32) * att_ref[:, cols].astype(F32)
        delta[h] = jnp.broadcast_to(jnp.sum(both.T, axis=0, keepdims=True), delta.shape[1:])
    zero = jnp.zeros((rows, hd), BF16)

    def put(b, keep, give):
        nz = keep_near.shape[0]
        z = lax.rem(lax.div(b, 2) - lax.div(scal[0], 2) + nz, nz)
        near = lax.rem(b, 2) == lax.rem(scal[0], 2)

        @pl.when(near)
        def _():
            keep_near[z] = keep
            give_near[z] = give

        @pl.when(jnp.logical_not(near))
        def _():
            keep_far[z] = keep
            give_far[z] = give

    def clear(b, carry):
        put(b, zero, zero)
        return carry

    start, stop = block_bounds(scal, rows)
    lax.fori_loop(0, start, clear, 0)
    lax.fori_loop(stop, 2 * keep_near.shape[0], clear, 0)

    def run(b, masked):
        kb, vb = key_value(scal, refs, b, rows)
        kt = kb.astype(F32).T.astype(BF16)
        dk = jnp.zeros((rows, hd), F32)
        dv = jnp.zeros((rows, hd), F32)
        for h in range(heads):
            cols = slice(h * hd, (h + 1) * hd)
            qh = q_ref[:, cols]
            dh = d_ref[:, cols]
            p = probs_t(scal, kb, qh, lo_ref[...], b, rows, factor, log_ref[h, 0:1, :], masked)
            dp = mm(vb, dh, 1, 1)
            ds = (p * (dp - delta[h, 0:1, :])).astype(BF16)
            dv += mm(p.astype(BF16), dh, 1, 0)
            dk += mm(ds, qh, 1, 0)
            acc[h] += mm(kt, ds, 1, 0)
        dk = (dk * scale).astype(BF16)
        dv = dv.astype(BF16)
        put(b, jnp.where(scal[3] == 0, dk, dv), jnp.where(scal[3] == 0, dv, dk))

    for_blocks(scal, rows, run)
    for h in range(heads):
        dq = (acc[h] * scale).T
        dq = dq * cos_ref[...] + pltpu.roll(dq, hd // 2, 1) * sin_ref[...]
        dq = dq.astype(BF16)
        dq_ref[:, h * hd : (h + 1) * hd] = dq
        bias_ref[:, h * hd : (h + 1) * hd] = jnp.sum(dq.astype(F32), axis=0, keepdims=True)


VMEM = pl.BlockSpec(memory_space=pltpu.VMEM)
SMEM = pl.BlockSpec(memory_space=pltpu.SMEM)
ANYWHERE = pl.BlockSpec(memory_space=pl.ANY)
MIB = 1024 * 1024


def cost(us):
    return pl.CostEstimate(flops=int(us * 1.15e9), bytes_accessed=0, transcendentals=0)


def attend(scal, q, kv, lo):
    rows, width = q.shape
    hd = kv[0].shape[2]
    heads = width // hd
    return pl.pallas_call(
        attend_kernel,
        in_specs=[SMEM] + [VMEM] * 6,
        out_specs=[VMEM, VMEM],
        out_shape=[
            jax.ShapeDtypeStruct((rows, width), BF16),
            jax.ShapeDtypeStruct((heads, 8, rows), F32),
        ],
        scratch_shapes=[pltpu.VMEM((heads, hd, rows), F32), pltpu.VMEM((heads, 8, rows), F32)],
        compiler_params=pltpu.CompilerParams(vmem_limit_bytes=20 * MIB),
        cost_estimate=cost(50),
        name="attend",
    )(scal, q, *kv, lo)


def attend_back(scal, q, kv, lo, att, logs, d_att, cos, sin):
    rows, width = q.shape
    hd = kv[0].shape[2]
    heads = width // hd
    grads = jax.ShapeDtypeStruct(kv[0].shape[:1] + (rows, hd), BF16)
    return pl.pallas_call(
        attend_back_kernel,
        in_specs=[SMEM] + [VMEM] * 11,
        out_specs=[VMEM] * 6,
        out_shape=[
            jax.ShapeDtypeStruct((rows, width), BF16),
            jax.ShapeDtypeStruct((1, width), F32),
            *([grads] * 4),
        ],
        scratch_shapes=[pltpu.VMEM((heads, hd, rows), F32), pltpu.VMEM((heads, 8, rows), F32)],
        compiler_params=pltpu.CompilerParams(vmem_limit_bytes=26 * MIB),
        cost_estimate=cost(8),
        name="attend_back",
    )(scal, q, *kv, lo, att, logs, d_att, cos, sin)


CHUNK = 512


def column_fetch(scal, quarters, nz, quarter, rows, normed, nbuf, nsem, cots=None, cbuf=None, csem=None):
    z, core, y = scal[1], lax.rem(scal[2], 2), lax.div(scal[2], 2)
    per_chunk = CHUNK // quarter
    chunks = [(k, first) for k in range(quarters) for first in range(0, nz, per_chunk)]

    def fetch(c):
        k, first = chunks[c]
        slot = c % nbuf.shape[0]
        q = 2 * ((1 - y) if k % 2 else y) + ((1 - core) if k // 2 else core)
        for i in range(per_chunk):
            dist = first + i
            row = pl.multiple_of(lax.rem(z - dist + nz, nz) * rows + q * quarter, quarter)
            place = pl.ds(i * quarter, quarter)
            pltpu.make_async_copy(normed.at[pl.ds(row, quarter), :], nbuf.at[slot, place, :], nsem.at[slot]).start()
            if cots is None:
                continue
            if dist == 0:
                source = cots[0].at[pl.ds(pl.multiple_of(q * quarter, quarter), quarter), :]
            else:
                source = cots[k + 1].at[pl.ds((dist - 1) * quarter, quarter), :]
            pltpu.make_async_copy(source, cbuf.at[slot, place, :], csem.at[slot]).start()

    for c in range(min(nbuf.shape[0], len(chunks))):
        fetch(c)
    return fetch, len(chunks)


def column_put(scal, acc, keep, give):
    nz, part, _ = keep.shape
    flat = acc[...].T.astype(BF16)
    for i in range(2 * nz):
        value = flat[i * part : (i + 1) * part, :]
        dist = lax.rem(i // 2 - scal[1] + nz, nz)

        @pl.when(scal[0] == i % 2)
        def _(value=value, dist=dist):
            keep[dist] = value

        @pl.when(scal[0] != i % 2)
        def _(value=value, dist=dist):
            give[dist] = value


def column_first_kernel(quarters, scal, normed, *refs):
    cots = refs[: quarters + 1]
    gate_ref, up_ref, down_ref, kd, gd, d_gate_ref, d_up_ref = refs[quarters + 1 : quarters + 8]
    nbuf, cbuf, ad, nsem, csem = refs[quarters + 8 :]
    rows = cots[0].shape[0]
    fetch, count = column_fetch(
        scal, quarters, kd.shape[0], rows // quarters, rows, normed, nbuf, nsem, cots, cbuf, csem
    )
    slots = nbuf.shape[0]
    for c in range(count):
        slot = c % slots
        place = slice(c * CHUNK, (c + 1) * CHUNK)
        pltpu.make_async_copy(nbuf.at[slot], nbuf.at[slot], nsem.at[slot]).wait()
        pltpu.make_async_copy(cbuf.at[slot], cbuf.at[slot], csem.at[slot]).wait()
        gate = mm(gate_ref[...], nbuf[slot], 1, 1)
        up = mm(up_ref[...], nbuf[slot], 1, 1)
        d_hidden = mm(down_ref[...], cbuf[slot], 1, 1)
        sig = 1.0 / (1.0 + jnp.exp(-gate))
        silu = gate * sig
        hidden = (silu * up).astype(BF16)
        d_gate_ref[:, place] = (d_hidden * up * sig * (1.0 + gate * (1.0 - sig))).astype(BF16)
        d_up_ref[:, place] = (d_hidden * silu).astype(BF16)
        grad = mm(hidden, cbuf[slot], 1, 0)
        ad[...] = grad if c == 0 else ad[...] + grad
        if c + slots < count:
            fetch(c + slots)
    column_put(scal, ad, kd, gd)


def column_second_kernel(quarters, rows, scal, normed, d_gate_ref, d_up_ref, kg, gg, ku, gu, nbuf, ag, au, nsem):
    fetch, count = column_fetch(scal, quarters, kg.shape[0], rows // quarters, rows, normed, nbuf, nsem)
    slots = nbuf.shape[0]
    for c in range(count):
        slot = c % slots
        place = slice(c * CHUNK, (c + 1) * CHUNK)
        pltpu.make_async_copy(nbuf.at[slot], nbuf.at[slot], nsem.at[slot]).wait()
        for acc, left in ((ag, d_gate_ref), (au, d_up_ref)):
            grad = mm(left[:, place], nbuf[slot], 1, 0)
            acc[...] = grad if c == 0 else acc[...] + grad
        if c + slots < count:
            fetch(c + slots)
    column_put(scal, ag, kg, gg)
    column_put(scal, au, ku, gu)


def column_first(scal, normed, cots, gate_s, up_s, down_s, n):
    unit, width = gate_s.shape
    quarters = len(cots) - 1
    tokens = normed.shape[0]
    slots = min(tokens // CHUNK, 4)
    out = jax.ShapeDtypeStruct((n // 2, width // n, unit), BF16)
    units = jax.ShapeDtypeStruct((unit, tokens), BF16)
    return pl.pallas_call(
        functools.partial(column_first_kernel, quarters),
        in_specs=[SMEM] + [ANYWHERE] * (quarters + 2) + [VMEM] * 3,
        out_specs=[VMEM] * 4,
        out_shape=[out] * 2 + [units] * 2,
        scratch_shapes=[pltpu.VMEM((slots, CHUNK, width), BF16)] * 2
        + [pltpu.VMEM((unit, width), F32)]
        + [pltpu.SemaphoreType.DMA((slots,))] * 2,
        compiler_params=pltpu.CompilerParams(vmem_limit_bytes=50 * MIB),
        cost_estimate=cost(14),
        name="column_first",
    )(scal, normed, *cots, gate_s, up_s, down_s)


def column_second(scal, normed, d_gate, d_up, rows, n):
    unit, tokens = d_gate.shape
    width = normed.shape[1]
    slots = min(tokens // CHUNK, 4)
    out = jax.ShapeDtypeStruct((n // 2, width // n, unit), BF16)
    return pl.pallas_call(
        functools.partial(column_second_kernel, 4, rows),
        in_specs=[SMEM, ANYWHERE, VMEM, VMEM],
        out_specs=[VMEM] * 4,
        out_shape=[out] * 4,
        scratch_shapes=[pltpu.VMEM((slots, CHUNK, width), BF16)]
        + [pltpu.VMEM((unit, width), F32)] * 2
        + [pltpu.SemaphoreType.DMA((slots,))],
        compiler_params=pltpu.CompilerParams(vmem_limit_bytes=40 * MIB),
        cost_estimate=cost(10),
        name="column_second",
    )(scal, normed, d_gate, d_up)


FF_STEPS = 4


def mlp_kernel(scal, n_ref, dh_ref, gate_ref, up_ref, hidden_ref, d_keep, d_give, d_acc):
    step = pl.program_id(0)
    gate = mm(gate_ref[...], n_ref[...], 1, 1)
    up = mm(up_ref[...], n_ref[...], 1, 1)
    d_hidden = dh_ref[...].astype(F32)
    sig = 1.0 / (1.0 + jnp.exp(-gate))
    silu = gate * sig
    hidden_ref[...] = (silu * up).astype(BF16)
    d_gate = (d_hidden * up * sig * (1.0 + gate * (1.0 - sig))).astype(BF16)
    d_up = (d_hidden * silu).astype(BF16)
    d_normed = mm(d_gate, gate_ref[...], 0, 0) + mm(d_up, up_ref[...], 0, 0)

    @pl.when(step == 0)
    def _():
        d_acc[...] = d_normed

    @pl.when(step > 0)
    def _():
        d_acc[...] += d_normed

    @pl.when(step == FF_STEPS - 1)
    def _():
        halves(scal[0], d_acc, d_keep, d_give)


def mlp(core, normed, d_hidden, gate_t, up_t):
    rows, width = normed.shape
    ff = gate_t.shape[0]
    units = pl.BlockSpec((ff // FF_STEPS, width), lambda i: (i, 0))
    tokens = pl.BlockSpec((ff // FF_STEPS, rows), lambda i: (i, 0))
    return pl.pallas_call(
        mlp_kernel,
        grid=(FF_STEPS,),
        in_specs=[SMEM, VMEM, tokens, units, units],
        out_specs=[tokens, VMEM, VMEM],
        out_shape=[
            jax.ShapeDtypeStruct((ff, rows), BF16),
            jax.ShapeDtypeStruct((rows // 2, width), F32),
            jax.ShapeDtypeStruct((rows // 2, width), BF16),
        ],
        scratch_shapes=[pltpu.VMEM((rows, width), F32)],
        compiler_params=pltpu.CompilerParams(vmem_limit_bytes=40 * MIB, dimension_semantics=("arbitrary",)),
        cost_estimate=cost(12),
        name="mlp",
    )(core.reshape(1).astype(jnp.int32), normed, d_hidden, gate_t, up_t)


def halves(core, total, keep, give):
    half = total.shape[0] // 2
    keep[...] = total[pl.ds(pl.multiple_of(core * half, half), half), :]
    give[...] = total[pl.ds(pl.multiple_of((1 - core) * half, half), half), :].astype(BF16)


def project_kernel(scal, *refs):
    count = len(refs) - 11
    ring, (cos_ref, sin_ref, q_ref, qw_ref, kvw_ref, n_ref) = refs[:count], refs[count : count + 6]
    kv_ref, sum_ref, keep, give, total = refs[count + 6 :]
    rows = q_ref.shape[0]
    d_kv = ring[0][0:rows, :].astype(F32)
    for piece in ring[1:]:
        d_kv += piece[0:rows, :].astype(F32)
    turned = d_kv * cos_ref[...] + pltpu.roll(d_kv, d_kv.shape[1] // 2, 1) * sin_ref[...]
    d_kv = jnp.where(scal[0] == 0, turned, d_kv).astype(BF16)
    kv_ref[...] = mm(n_ref[...], d_kv, 0, 0).astype(BF16)
    sum_ref[...] = jnp.sum(d_kv.astype(F32), axis=0, keepdims=True)
    total[...] = mm(q_ref[...], qw_ref[...], 1, 1) + mm(d_kv, kvw_ref[...], 1, 1)
    halves(scal[0], total, keep, give)


def output_kernel(scal, h_ref, down_ref, keep, give, total):
    total[...] = mm(h_ref[...], down_ref[...], 0, 0)
    halves(scal[0], total, keep, give)


def halves_shapes(rows, width):
    return [jax.ShapeDtypeStruct((rows // 2, width), F32), jax.ShapeDtypeStruct((rows // 2, width), BF16)]


def project(core, ring, cos, sin, d_query, q_weight, kv_cols, normed):
    rows, width = d_query.shape[0], q_weight.shape[0]
    return pl.pallas_call(
        project_kernel,
        in_specs=[SMEM] + [VMEM] * (len(ring) + 6),
        out_specs=[VMEM] * 4,
        out_shape=[
            jax.ShapeDtypeStruct((width, ring[0].shape[1]), BF16),
            jax.ShapeDtypeStruct((1, ring[0].shape[1]), F32),
            *halves_shapes(rows, width),
        ],
        scratch_shapes=[pltpu.VMEM((rows, width), F32)],
        compiler_params=pltpu.CompilerParams(vmem_limit_bytes=24 * MIB),
        cost_estimate=cost(30),
        name="project",
    )(core.reshape(1).astype(jnp.int32), *ring, cos, sin, d_query, q_weight, kv_cols, normed)


def project_output(core, hidden, down):
    rows, width = hidden.shape[1], down.shape[1]
    return pl.pallas_call(
        output_kernel,
        in_specs=[SMEM] + [VMEM] * 2,
        out_specs=[VMEM] * 2,
        out_shape=halves_shapes(rows, width),
        scratch_shapes=[pltpu.VMEM((rows, width), F32)],
        compiler_params=pltpu.CompilerParams(vmem_limit_bytes=30 * MIB),
        cost_estimate=cost(30),
        name="project_output",
    )(core.reshape(1).astype(jnp.int32), hidden, down)


def norm_back_kernel(x_ref, gain_ref, dn_ref, base_ref, dx_ref, gain_grad_ref):
    values = x_ref[...].astype(F32)
    factor = lax.rsqrt(jnp.mean(values * values, axis=-1, keepdims=True) + RMS_EPS)
    w = values * factor
    dn = dn_ref[...].astype(F32)
    gain_grad_ref[...] = jnp.sum(dn * w, axis=0, keepdims=True)
    dg = dn * gain_ref[...].astype(F32)
    dx_ref[...] = base_ref[...] + factor * (dg - w * jnp.mean(dg * w, axis=-1, keepdims=True))


def norm_back(x, gain, dn, base):
    rows, width = x.shape
    return pl.pallas_call(
        norm_back_kernel,
        in_specs=[VMEM] * 4,
        out_specs=[VMEM] * 2,
        out_shape=[jax.ShapeDtypeStruct((rows, width), F32), jax.ShapeDtypeStruct((1, width), F32)],
        compiler_params=pltpu.CompilerParams(vmem_limit_bytes=24 * MIB),
        cost_estimate=cost(30),
        name="norm_back",
    )(x, gain.reshape(1, width), dn, base)


def assemble_kernel(nz, scal, *refs):
    unit = refs[0].shape[1]
    groups, targets = (refs[:nz], refs[nz : 2 * nz], refs[2 * nz : 3 * nz]), refs[3 * nz :]

    def block(group, j):
        dist = lax.rem(scal[1] - j + nz, nz)
        value = group[0][...]
        for d in range(1, nz):
            value = jnp.where(dist == d, group[d][...], value)
        return value.astype(F32)

    for group, target in zip(groups, targets):
        target[...] = jnp.concatenate([block(group, j) for j in range(nz)], axis=1)


def assemble(scal, gate, up, down):
    nz = len(gate)
    part, unit = gate[0].shape
    ff = nz * unit
    return pl.pallas_call(
        functools.partial(assemble_kernel, nz),
        in_specs=[SMEM] + [VMEM] * (3 * nz),
        out_specs=[VMEM] * 3,
        out_shape=[jax.ShapeDtypeStruct((part, ff), F32)] * 3,
        compiler_params=pltpu.CompilerParams(vmem_limit_bytes=28 * MIB),
        cost_estimate=cost(30),
        name="assemble",
    )(scal, *gate, *up, *down)


def per_device(
    layer_input,
    segment_ids,
    positions,
    attn_gain,
    q_weight,
    q_bias,
    kv_weight,
    kv_bias,
    o_weight,
    mlp_gain,
    gate_weight,
    up_weight,
    down_weight,
    cotangent,
):
    rows, width = layer_input.shape
    heads, hd = q_bias.shape
    ff = gate_weight.shape[1]
    nz, x, y, core = lax.axis_size("z"), lax.axis_index("x"), lax.axis_index("y"), lax.axis_index("core")
    z = lax.axis_index("z")
    n, ntp = 2 * nz, 4
    ctx = 2 * z + x
    tp = 2 * y + core
    unit = ff // nz

    o_full = jnp.concatenate(gather_tp(o_weight, core, y), axis=0)
    gate_s = lax.dynamic_slice_in_dim(gate_weight.T, z * unit, unit, 0)
    up_s = lax.dynamic_slice_in_dim(up_weight.T, z * unit, unit, 0)
    down_s = lax.dynamic_slice_in_dim(down_weight, z * unit, unit, 0)

    inputs = layer_input.astype(F32)
    gain_one = attn_gain.astype(F32)
    factor_one = lax.rsqrt(jnp.mean(inputs * inputs, axis=-1, keepdims=True) + RMS_EPS)
    normed = (inputs * factor_one * gain_one).astype(BF16)
    cosine, sine = rope_tables(positions, hd)
    cos_back = jnp.concatenate([cosine, cosine], axis=1)
    sin_back = jnp.concatenate([sine, -sine], axis=1)
    query = mm(normed, q_weight, 1, 0) + q_bias.astype(F32).reshape(-1)
    query_rot = rotate(query.reshape(rows, heads, hd), cosine[:, None], sine[:, None])
    query_rot = query_rot.astype(BF16).reshape(rows, heads * hd)
    column = (2 * core + y) * hd
    kv_cols = lax.dynamic_slice_in_dim(kv_weight, column, hd, 1)
    kv_own_bias = lax.dynamic_slice_in_dim(kv_bias, column, hd, 0).astype(F32)
    kv_own = mm(normed, kv_cols, 1, 0) + kv_own_bias
    kv_own = jnp.where(core == 0, rotate(kv_own, cosine, sine), kv_own).astype(BF16)

    ids = segment_ids.astype(BF16).reshape(rows // hd, hd)
    ids = jnp.pad(ids, ((0, EXTRA - rows // hd), (0, 0)))
    packed = jnp.concatenate([kv_own, ids], axis=0)
    near = lax.all_to_all(
        jnp.broadcast_to(packed[None], (nz,) + packed.shape), "z", split_axis=0, concat_axis=0, tiled=True
    )
    quarter = rows // ntp
    cot_own = lax.dynamic_slice_in_dim(after(cotangent, near), tp * quarter, quarter, 0)
    cot_ahead = [along_z(cot_own, 1)]
    far = swap(near, "x")
    kv = (near, far, swap(near, "core"), swap(far, "core"))
    kv, gate_s, up_s, down_s = lax.optimization_barrier((kv, gate_s, up_s, down_s))
    all_ids = jnp.stack([near[:, rows : rows + rows // hd], far[:, rows : rows + rows // hd]]).astype(F32)
    starts = [jnp.sum((all_ids < k).astype(F32)).astype(jnp.int32) for k in (1, 2, 3)]
    lo = jnp.where(
        segment_ids == 0,
        0,
        jnp.where(segment_ids == 1, starts[0], jnp.where(segment_ids == 2, starts[1], starts[2])),
    )
    scal = jnp.stack([ctx, lo[0], lo[-1], core]).astype(jnp.int32)
    lo = lo.reshape(1, rows)

    attended, logs = attend(scal, query_rot, kv, lo)
    attended, logs, cot_ahead = lax.optimization_barrier((attended, logs, cot_ahead))
    cot_ahead += [along_z(cot_ahead[-1], 1)]
    d_hidden = mm(down_weight, after(cotangent, attended), 1, 1).astype(BF16)
    attended_all = jnp.concatenate(gather_tp(attended, core, y), axis=1)
    attended_all, d_hidden, cot_ahead = lax.optimization_barrier((attended_all, d_hidden, cot_ahead))
    while len(cot_ahead) < nz - 1:
        cot_ahead += [along_z(cot_ahead[-1], 1)]
    hidden_in = inputs + mm(attended_all, o_full, 1, 0)

    gain_two = mlp_gain.astype(F32)
    factor_two = lax.rsqrt(jnp.mean(hidden_in * hidden_in, axis=-1, keepdims=True) + RMS_EPS)
    normed_two = (hidden_in * factor_two * gain_two).astype(BF16)
    normed_all = column_tokens(normed_two, core)

    hidden, d_keep, d_give = mlp(core, normed_two, d_hidden, gate_weight.T, up_weight.T)
    hidden, d_keep, d_give, cot_ahead = lax.optimization_barrier((hidden, d_keep, d_give, cot_ahead))
    d_half = sum_y(sum_core(d_keep, d_give))
    cot_here = jnp.concatenate(after(cot_ahead, d_half), axis=0)
    cot_there = swap(cot_here, "y")
    d_normed_two = join_core(d_half, core).astype(F32)

    w_two = hidden_in * factor_two
    part_mlp_gain = jnp.sum(d_normed_two * w_two, axis=0)
    dg_two = d_normed_two * gain_two
    d_hidden_in = cotangent.astype(F32) + factor_two * (
        dg_two - w_two * jnp.mean(dg_two * w_two, axis=-1, keepdims=True)
    )
    d_attn = d_hidden_in.astype(BF16)
    d_attended = mm(d_attn, o_weight, 1, 1).astype(BF16)
    part, small = width // n, width // (n * ntp)
    g_o = mm(d_attn, attended, 0, 0).astype(BF16).reshape(nz, 2, part, heads * hd).swapaxes(0, 1)
    keep_o = lax.dynamic_index_in_dim(g_o, x, 0, keepdims=False)
    give_o = lax.dynamic_index_in_dim(g_o, 1 - x, 0, keepdims=False)
    d_attended, keep_o, give_o = lax.optimization_barrier((d_attended, keep_o, give_o))
    came_o = swap(give_o, "x")

    back = attend_back(scal, query_rot, kv, lo, attended, logs, d_attended, cos_back, sin_back)
    back, came_o, cot_there = lax.optimization_barrier((back, came_o, cot_there))
    d_query, q_bias_sum, keep_near, keep_far, give_near, give_far = back
    cots = (cotangent, cot_here, cot_there, swap(cot_here, "core"), swap(cot_there, "core"))
    d_far = (keep_far.astype(F32) + swap(give_far, "core").astype(F32)).astype(BF16)
    came_near = swap(give_near, "core")
    g_q = mm(normed, after(d_query, d_far), 0, 0).astype(BF16).reshape(nz, 2, part, heads * hd)
    keep_q = lax.dynamic_index_in_dim(g_q, x, 1, keepdims=False)
    give_q = lax.dynamic_index_in_dim(g_q, 1 - x, 1, keepdims=False)
    g_o = by_distance((keep_o.astype(F32) + came_o.astype(F32)).astype(BF16), z)
    came_near, d_far, keep_q, give_q, g_o, normed_all, cots = lax.optimization_barrier(
        (came_near, d_far, keep_q, give_q, g_o, normed_all, cots)
    )
    came_far, came_q, g_o = swap(d_far, "x"), swap(give_q, "x"), spread(g_o)

    place = jnp.stack([x, z, tp]).astype(jnp.int32)
    keep_down, give_down, d_gate_c, d_up_c = column_first(place, normed_all, cots, gate_s, up_s, down_s, n)
    came_far, came_q, g_o, d_gate_c, give_down = lax.optimization_barrier((came_far, came_q, g_o, d_gate_c, give_down))
    ring = [
        (keep_near[s].astype(F32) + came_near[s].astype(F32) + came_far[s].astype(F32)).astype(BF16)
        for s in range(nz)
    ]
    g_q = by_distance((keep_q.astype(F32) + came_q.astype(F32)).astype(BF16), z)
    ring = [
        jnp.concatenate([ring[s]] + [g_q[s][:, h * hd : (h + 1) * hd] for h in range(heads)], axis=0)
        for s in range(nz)
    ]
    ring, d_gate_c = lax.optimization_barrier((ring, d_gate_c))
    ring = spread(ring)
    came_down = swap(give_down, "x")
    keep_gate, give_gate, keep_up, give_up = column_second(place, normed_all, d_gate_c, d_up_c, rows, n)
    came_down, ring, give_gate, give_up = lax.optimization_barrier((came_down, ring, give_gate, give_up))

    sums, give_gate, ring = lax.optimization_barrier((sum_parts(keep_down, came_down), give_gate, ring))
    came_gate, g_down = swap(give_gate, "x"), spread(sums)
    parts = project(core, ring, cos_back, sin_back, d_query, q_weight, kv_cols, normed)
    parts, came_gate, g_down = lax.optimization_barrier((parts, came_gate, g_down))
    g_kv, d_kv_sum = parts[0].reshape(n * ntp, small, hd), parts[1]
    sums, give_up, parts = lax.optimization_barrier((sum_parts(keep_gate, came_gate), give_up, parts))
    came_up, g_gate = swap(give_up, "x"), spread(sums)
    d_half = sum_core(*parts[2:])
    hidden, d_half = lax.optimization_barrier((hidden, d_half))
    came_half = swap(d_half, "y")
    o_parts = project_output(core, hidden, down_weight)
    o_parts, came_up, g_gate, came_half = lax.optimization_barrier((o_parts, came_up, g_gate, came_half))
    d_normed = (d_half.astype(F32) + came_half.astype(F32)).astype(BF16)
    sums, d_normed, o_parts = lax.optimization_barrier((sum_parts(keep_up, came_up), d_normed, o_parts))
    g_up = spread(sums)
    o_half = sum_core(*o_parts)
    d_normed = join_core(d_normed, core)
    d_normed, o_half = lax.optimization_barrier((d_normed, o_half))
    came_o_half = swap(o_half, "y")
    dx, part_attn_gain = norm_back(layer_input, attn_gain, d_normed, d_hidden_in)
    dx, part_attn_gain, g_up, came_o_half = lax.optimization_barrier((dx, part_attn_gain, g_up, came_o_half))
    o_half = (o_half.astype(F32) + came_o_half.astype(F32)).astype(BF16)
    output = (hidden_in + join_core(o_half, core).astype(F32)).astype(BF16)

    bias_cols = hd // n
    tail_rows = jnp.concatenate(
        [
            jnp.broadcast_to(d_kv_sum, (n, hd)),
            part_mlp_gain.reshape(n, part),
            part_attn_gain.reshape(n, part),
            jnp.broadcast_to(q_bias_sum, (n, heads * hd)),
        ],
        axis=1,
    )
    extra = -(-tail_rows.shape[1] // (EXTRA * hd)) * EXTRA
    tail_rows = jnp.pad(tail_rows, ((0, 0), (0, extra * hd - tail_rows.shape[1]))).astype(BF16)
    tail_rows = jnp.broadcast_to(tail_rows.reshape(n, 1, extra, hd), (n, ntp, extra, hd)).reshape(-1, extra, hd)
    g_kv = lax.all_to_all(
        jnp.concatenate([g_kv, tail_rows], axis=1), ("z", "x", "y", "core"), split_axis=0, concat_axis=0, tiled=True
    )
    g_gate, g_up, g_down = assemble(place, g_gate, g_up, g_down)
    g_gate, g_up, g_down, g_kv = lax.optimization_barrier((g_gate, g_up, g_down, g_kv))
    g_kv = jnp.sum(g_kv.reshape(n, ntp, small + extra, hd).astype(F32), axis=0)
    sums = lax.dynamic_index_in_dim(g_kv[:, small:], tp, 0, keepdims=False).reshape(-1)[hd:]
    g_mlp_gain = sums[:part]
    g_attn_gain = sums[part : 2 * part]
    g_q_bias = sums[2 * part : 2 * part + heads * hd].reshape(heads, hd)
    g_q_bias = lax.dynamic_slice_in_dim(g_q_bias, ctx * bias_cols, bias_cols, 1)
    g_kv = jnp.concatenate([g_kv[0], g_kv[2], g_kv[1], g_kv[3]], axis=1)
    bias_size = kv_bias.shape[0] // (n * ntp)
    g_kv_bias = lax.dynamic_slice_in_dim(g_kv[small], (ctx * ntp + tp) * bias_size, bias_size, 0)
    g_kv = g_kv[:small]

    g_down = g_down.T
    g_o = sum(g.astype(F32) for g in after(g_o, dx)).T
    g_q = sum(r[rows:].astype(F32) for r in after(ring, dx)).reshape(heads, part, hd).transpose(1, 0, 2).reshape(part, heads * hd)

    return (
        output,
        dx,
        g_attn_gain,
        g_q,
        g_q_bias,
        g_kv,
        g_kv_bias,
        g_o,
        g_mlp_gain,
        g_gate,
        g_up,
        g_down,
    )


def solution(mesh):
    n, ntp = mesh.shape["ctx"], mesh.shape["tp"]
    fine = jax.sharding.Mesh(mesh.devices.reshape(n // 2, 2, ntp // 2, 2), ("z", "x", "y", "core"))
    ctx, tp = ("z", "x"), ("y", "core")
    both = ctx + tp
    return jax.shard_map(
        per_device,
        mesh=fine,
        in_specs=(
            P(ctx, None),
            P(ctx),
            P(ctx),
            P(),
            P(None, tp),
            P(tp, None),
            P(),
            P(),
            P(tp, None),
            P(),
            P(None, tp),
            P(None, tp),
            P(tp, None),
            P(ctx, None),
        ),
        out_specs=(
            P(ctx, None),
            P(ctx, None),
            P(ctx),
            P(ctx, tp),
            P(tp, ctx),
            P(both, None),
            P(both),
            P(tp, ctx),
            P(ctx),
            P(ctx, tp),
            P(ctx, tp),
            P(tp, ctx),
        ),
        check_vma=False,
    )
```
